32 devices in a mesh: rows: 8 (over z, y), cols: 2 (over x), dp: 2 (over core).
Axes of the slice: x: 2, y: 2, z: 4, core: 2. Of those that a mesh axis runs over, the one named last changes fastest.
Arguments:
- queries: bfloat16 [2, 128, 32, 1024], P('dp', 'rows', 'cols'), may hold values from -69 to 69
- keys_values: bfloat16 [2, 2, 128, 32, 1024], P(None, 'dp', 'rows', 'cols'), may hold values from -6 to 6
- out_weight: bfloat16 [1024, 1024], replicated, may hold values from -0.1875 to 0.1875
- out_grad: bfloat16 [2, 128, 32, 1024], P('dp', 'rows', 'cols'), may hold values from -6 to 6
Outputs:
- attn_out: bfloat16 [2, 128, 32, 1024], P('dp', 'rows', 'cols')
- query_grad: bfloat16 [2, 128, 32, 1024], P('dp', 'rows', 'cols')
- kv_grad: bfloat16 [2, 2, 128, 32, 1024], P(None, 'dp', 'rows', 'cols')
- weight_grad: float32 [1024, 1024], P('rows', ('cols', 'dp'))
The draws below stay inside these ranges and needn't reach their ends.
All inputs are finite; a program needn't handle non-finite values.
Results may differ from the reference program's by a relative error of at most 0.012.
The reference program's roundings to bfloat16 on the way count: a program that leaves them out, or rounds other values in their place, can miss the bound.
Values may be sent and summed in bfloat16 or wider, within the bound.
A program may use at most 128 MiB of HBM per device.

```python
import math
import jax
import jax.numpy as jnp
from jax import lax

D = 1024
NH = 16
HD = 64
RAD = 6
WIN = 13
QB = 8
TW = 16
B = 2
HH = 128
WW = 32
TOKENS = 8192


def paired_fields(key):
    shape = (B, HH, WW, NH, HD)
    key_q = jax.random.fold_in(key, 11)
    key_k = jax.random.fold_in(key, 12)
    key_v = jax.random.fold_in(key, 15)
    queries = jnp.clip(jax.random.normal(key_q, shape, jnp.float32), -6.0, 6.0)
    keys = jnp.clip(jax.random.normal(key_k, shape, jnp.float32), -6.0, 6.0)
    values = jnp.clip(jax.random.normal(key_v, shape, jnp.float32), -6.0, 6.0)
    flat = (B, HH, WW, D)
    return (queries.reshape(flat), keys.reshape(flat), values.reshape(flat))


def draw_queries(key, part):
    return paired_fields(key)[0].astype(jnp.bfloat16)


def draw_keys_values(key, part):
    fields = paired_fields(key)
    return jnp.stack((fields[1], fields[2])).astype(jnp.bfloat16)


def with_spikes(array, own_key, source, target, shards_of, factor):
    owner, partner = [(jnp.arange(array.shape[position]) // (array.shape[position] // shards_of)).reshape([-1 if axis == position else 1 for axis in range(array.ndim)]) for position in (source, target)]
    chosen = jax.random.permutation(own_key, shards_of)[partner]
    strong = (owner == chosen) | (owner == (partner + shards_of // 2) % shards_of)
    return jnp.where(strong, factor * array, array)


def block_levels(rng, dims, shards, low, top_value):
    def one(axis_at, blocks):
        draws = jax.random.uniform(jax.random.fold_in(jax.random.fold_in(rng, 6), axis_at), (blocks,), jnp.float32, low / len(shards), top_value / len(shards))
        return jnp.repeat(jnp.exp(draws), dims[axis_at] // blocks).reshape((-1,) + (1,) * (len(dims) - axis_at - 1))

    gain = one(*shards[0])
    for cut in shards[1:]:
        gain = gain * one(*cut)
    return gain


def centred(rng, extent, spread, bound, split=(), kind=jnp.bfloat16):
    array = spread * jax.random.normal(rng, extent, jnp.float32)
    if split:
        array = array * block_levels(rng, extent, split, -0.22, 0.18)
    return jnp.clip(array, -bound, bound).astype(kind)


def bell_draw_with(stream_key, dims, scale, most, split, heavy, kind=jnp.bfloat16):
    result = scale * jax.random.normal(stream_key, dims, jnp.float32)
    if split:
        result = result * block_levels(stream_key, dims, split, -0.22, 0.18)
    return jnp.clip(with_spikes(result, jax.random.fold_in(stream_key, 3), *heavy), -most, most).astype(kind)


def setup_inputs(seed: int = 0) -> dict:
    seeds = jax.random.split(jax.random.key(seed), 5)
    queries = draw_queries(jax.random.fold_in(seeds[4], 71), 0)
    keys_values = draw_keys_values(jax.random.fold_in(seeds[4], 71), 0)
    out_weight = centred(seeds[2], (D, D), D ** -0.5, 0.1875)
    out_grad = bell_draw_with(seeds[3], (B, HH, WW, D), 1.0, 6.0, ((0, 2), (1, 8), (2, 2)), (1, 3, 8, 2.0))
    return dict(queries=queries, keys_values=keys_values, out_weight=out_weight, out_grad=out_grad)


def index_of(*entries):
    return tuple((jnp.asarray(e).astype(jnp.int32) for e in entries))

def window_mask(query_rows, query_cols, key_rows, key_cols, image_h, image_w):
    start_r = jnp.clip(query_rows - RAD, 0, image_h - WIN)
    start_c = jnp.clip(query_cols - RAD, 0, image_w - WIN)
    rows_ok = (key_rows[None, :] >= start_r[:, None]) & (key_rows[None, :] < start_r[:, None] + WIN)
    cols_ok = (key_cols[None, :] >= start_c[:, None]) & (key_cols[None, :] < start_c[:, None] + WIN)
    mask = rows_ok[:, None, :, None] & cols_ok[None, :, None, :]
    return mask.reshape(query_rows.shape[0] * query_cols.shape[0], key_rows.shape[0] * key_cols.shape[0])

def block_core(q_blk, k_blk, v_blk, do_blk, mask):
    scale = 1.0 / math.sqrt(HD)
    q_f = q_blk.astype(jnp.float32).reshape(-1, NH, HD)
    k_f = k_blk.astype(jnp.float32).reshape(-1, NH, HD)
    v_f = v_blk.astype(jnp.float32).reshape(-1, NH, HD)
    do_f = do_blk.astype(jnp.float32).reshape(-1, NH, HD)
    scores = jnp.einsum('qhd,khd->hqk', q_f, k_f) * scale
    scores = jnp.where(mask[None], scores, -jnp.inf)
    top = lax.optimization_barrier(jnp.max(scores, axis=2, keepdims=True))
    expd = jnp.exp(scores - top)
    probs = expd / lax.optimization_barrier(jnp.sum(expd, axis=2, keepdims=True))
    low = lax.optimization_barrier(probs.astype(jnp.bfloat16))
    att = lax.optimization_barrier(jnp.einsum('hqk,khd->qhd', low.astype(jnp.float32), v_f).astype(jnp.bfloat16))
    delta = lax.optimization_barrier(jnp.sum(do_f * att.astype(jnp.float32), axis=2))
    dprob = jnp.einsum('qhd,khd->hqk', do_f, v_f)
    dlow = lax.optimization_barrier((probs * (dprob - delta.T[:, :, None]) * scale).astype(jnp.bfloat16))
    dq = jnp.einsum('hqk,khd->qhd', dlow.astype(jnp.float32), k_f).astype(jnp.bfloat16)
    dk = jnp.einsum('hqk,qhd->khd', dlow.astype(jnp.float32), q_f)
    dv = jnp.einsum('hqk,qhd->khd', low.astype(jnp.float32), do_f)
    width = q_blk.shape[1]
    return (att.reshape(-1, width), dq.reshape(-1, width), dk.reshape(-1, width), dv.reshape(-1, width))

def one_image(queries, keys, values, out_grad, out_weight):
    key_pad = jnp.pad(keys, ((RAD, RAD), (RAD, RAD), (0, 0)))
    val_pad = jnp.pad(values, ((RAD, RAD), (RAD, RAD), (0, 0)))
    grad_rows = out_grad.reshape(-1, D)
    d_att = jnp.dot(grad_rows, out_weight.T, preferred_element_type=jnp.float32).astype(jnp.bfloat16).reshape(HH, WW, D)
    row_blocks = HH // QB
    col_blocks = WW // TW
    key_h = QB + 2 * RAD
    key_w = TW + 2 * RAD

    def step(accum, index):
        row = (index // col_blocks * QB).astype(jnp.int32)
        col = (index % col_blocks * TW).astype(jnp.int32)
        lower = jnp.clip(row - RAD, 0, HH - QB - 2 * RAD).astype(jnp.int32)
        q_blk = lax.dynamic_slice(queries, index_of(row, col, 0), (QB, TW, D)).reshape(-1, D)
        do_blk = lax.dynamic_slice(d_att, index_of(row, col, 0), (QB, TW, D)).reshape(-1, D)
        k_blk = lax.dynamic_slice(key_pad, index_of(lower + RAD, col, 0), (key_h, key_w, D)).reshape(-1, D)
        v_blk = lax.dynamic_slice(val_pad, index_of(lower + RAD, col, 0), (key_h, key_w, D)).reshape(-1, D)
        mask = window_mask(row + jnp.arange(QB, dtype=jnp.int32), col + jnp.arange(TW, dtype=jnp.int32), lower + jnp.arange(key_h, dtype=jnp.int32), col - RAD + jnp.arange(key_w, dtype=jnp.int32), HH, WW)
        att, dq, dk, dv = block_core(q_blk, k_blk, v_blk, do_blk, mask)
        older = lax.dynamic_slice(accum, index_of(0, lower + RAD, col, 0), (2, key_h, key_w, D))
        newer = older + jnp.stack((dk, dv)).reshape(2, key_h, key_w, D)
        accum = lax.dynamic_update_slice(accum, newer, index_of(0, lower + RAD, col, 0))
        return (accum, (att, dq))
    start = jnp.zeros((2, HH + 2 * RAD, WW + 2 * RAD, D), jnp.float32)
    accum, (att_blocks, dq_blocks) = lax.scan(step, start, jnp.arange(row_blocks * col_blocks, dtype=jnp.int32))
    attended = att_blocks.reshape(row_blocks, col_blocks, QB, TW, D).transpose(0, 2, 1, 3, 4).reshape(HH, WW, D)
    query_grad = dq_blocks.reshape(row_blocks, col_blocks, QB, TW, D).transpose(0, 2, 1, 3, 4).reshape(HH, WW, D)
    kv_grad = accum[:, RAD:RAD + HH, RAD:RAD + WW].astype(jnp.bfloat16)
    flat_att = attended.reshape(-1, D)
    attn_out = jnp.dot(flat_att, out_weight, preferred_element_type=jnp.float32).astype(jnp.bfloat16).reshape(HH, WW, D)
    weight_term = jnp.dot(flat_att.T, grad_rows, preferred_element_type=jnp.float32)
    return (attn_out, query_grad, kv_grad, weight_term)

def reference(queries, keys_values, out_weight, out_grad):
    results = [one_image(queries[b], keys_values[0, b], keys_values[1, b], out_grad[b], out_weight) for b in range(B)]
    attn_out = jnp.stack([r[0] for r in results])
    query_grad = jnp.stack([r[1] for r in results])
    kv_grad = jnp.stack([r[2] for r in results], axis=1)
    total = results[0][3]
    for r in results[1:]:
        total = total + r[3]
    weight_grad = total * (1.0 / math.sqrt(TOKENS))
    return (attn_out, query_grad, kv_grad, weight_grad)
```

```python
import functools
import math

import jax
import jax.numpy as jnp
from jax import lax
from jax.experimental import pallas as pl
from jax.experimental.pallas import tpu as pltpu
from jax.sharding import PartitionSpec as P

NH = 16
HD = 64
RAD = 6
WIN = 13
QB = 8
PAIR = 2 * HD
CHUNK = 1
CORNER = -(-2 * RAD * RAD // 16) * 16
NEAR = -(-RAD * RAD // 16) * 16
MESH = pl.DeviceIdType.MESH
F32 = jnp.float32
BF16 = jnp.bfloat16


def mm(a, b, ca, cb):
    return lax.dot_general(a, b, (((ca,), (cb,)), ((), ())), preferred_element_type=F32)


def kernel(
    tile_h, tile_w, n_rows, n_cols, n_dp,
    q_ref, kv_ref, w_ref, og_ref,
    out_ref, dq_ref, kvg_ref, wg_ref,
    main, side, own_side, acc, sacc, bias, att_t, d_att,
    rim_out, rim_in, srim_out, srim_in,
    slab, slab_low, got_dp, low_rows, got_rows, got_cols,
    halo_sems, mid_sems, corner_sems, rim_sems, srim_sems, dp_sems, rows_sems, cols_sems,
):
    sides = side.shape[0]
    blocks = tile_h // QB
    tokens = tile_h * tile_w
    width = q_ref.shape[1]
    pairs = width // PAIR
    edge = RAD * tile_w
    span = (QB + 2 * RAD) * tile_w
    mid = tile_h * RAD
    sspan = NEAR + mid
    step = QB * tile_w
    image_h, image_w = tile_h * n_rows, tile_w * n_cols
    scale = 1.0 / math.sqrt(HD)
    r, c, d = lax.axis_index("rows"), lax.axis_index("cols"), lax.axis_index("dp")
    chunks = pairs // CHUNK
    part = CHUNK * PAIR
    ways = (-1, 1)

    def lanes_of(g):
        return pl.ds(g * part, part)

    def row_there(way):
        return r > 0 if way < 0 else r < n_rows - 1

    def side_there(s):
        if sides == 1:
            return None
        return c > 0 if s == 0 else c < n_cols - 1

    def guarded(ok, action):
        if ok is None:
            action()
        else:
            pl.when(ok)(action)

    def side_col(s):
        return 1 - c if sides == 1 else c + (2 * s - 1)

    def slot(s):
        return 0 if sides == 1 else 1 - s

    def starts_at(s):
        if sides == 1:
            return (1 - c) * (tile_w - RAD)
        return 0 if s == 0 else tile_w - RAD

    barrier = pltpu.get_barrier_semaphore()
    for k in range(1, n_rows):
        pl.semaphore_signal(barrier, 1, device_id={"rows": lax.rem(r + k, n_rows)}, device_id_type=MESH)
    for k in range(1, n_cols):
        pl.semaphore_signal(barrier, 1, device_id={"cols": lax.rem(c + k, n_cols)}, device_id_type=MESH)
    for k in range(1, n_dp):
        pl.semaphore_signal(barrier, 1, device_id={"dp": lax.rem(d + k, n_dp)}, device_id_type=MESH)

    def rim_place(token, s):
        lower = token >= RAD * RAD
        cell = jnp.where(lower, token - RAD * RAD, token)
        row = (cell * 10923) >> 16
        place = row * tile_w + cell - row * RAD + starts_at(s) + jnp.where(lower, edge, 0)
        return jnp.where(token < 2 * RAD * RAD, place, -1)

    def own_place(token, s):
        row = (token * 10923) >> 16
        return row * tile_w + token - row * RAD + starts_at(s)

    def one_hot(place, shape, s, token_axis):
        token = lax.broadcasted_iota(jnp.int32, shape, token_axis)
        cell = lax.broadcasted_iota(jnp.int32, shape, 1 - token_axis)
        return (place(token, s) == cell).astype(F32).astype(BF16)

    pick_rim = [one_hot(rim_place, (CORNER, 2 * edge), s, 0) for s in range(sides)]
    put_rim = [one_hot(rim_place, (2 * edge, CORNER), s, 1) for s in range(sides)]
    put_own = [one_hot(own_place, (tokens, mid), s, 1) for s in range(sides)]
    for s in range(sides):
        chosen = one_hot(own_place, (mid, tokens), s, 0)
        for k in range(2):
            own_side[s, k, CORNER:] = mm(chosen, kv_ref[k], 1, 0).astype(BF16)

    pl.semaphore_wait(barrier, n_rows + n_cols + n_dp - 3)

    def row_link(way, src, dst, sems, g):
        i = 0 if way < 0 else 1
        return pltpu.make_async_remote_copy(
            src_ref=src, dst_ref=dst, send_sem=sems.at[0, i, g], recv_sem=sems.at[1, 1 - i, g],
            device_id={"rows": r + way}, device_id_type=MESH,
        )

    def row_arrival(way, dst, sems, g):
        i = 0 if way < 0 else 1
        return pltpu.make_async_remote_copy(
            src_ref=dst, dst_ref=dst, send_sem=sems.at[0, i, g], recv_sem=sems.at[1, i, g],
            device_id={"rows": r + way}, device_id_type=MESH,
        )

    def halo_place(way, at):
        return main.at[:, pl.ds(0 if way < 0 else edge + tokens, edge), at]

    def halo_copy(way, g):
        at = lanes_of(g)
        own = kv_ref.at[:, pl.ds(0 if way < 0 else tokens - edge, edge), at]
        return row_link(way, own, halo_place(-way, at), halo_sems, g)

    def halo_arrival(way, g):
        return row_arrival(way, halo_place(way, lanes_of(g)), halo_sems, g)

    def rim_copy(way, g):
        i = 0 if way < 0 else 1
        at = lanes_of(g)
        return row_link(way, rim_out.at[i, :, :, at], rim_in.at[1 - i, :, :, at], rim_sems, g)

    def rim_arrival(way, g):
        i = 0 if way < 0 else 1
        return row_arrival(way, rim_in.at[i, :, :, lanes_of(g)], rim_sems, g)

    def side_copy(s, src, dst, sems, g, at):
        return pltpu.make_async_remote_copy(
            src_ref=src.at[s, :, at, lanes_of(g)], dst_ref=dst.at[slot(s), :, at, lanes_of(g)],
            send_sem=sems.at[0, s, g], recv_sem=sems.at[1, slot(s), g],
            device_id={"cols": side_col(s)}, device_id_type=MESH,
        )

    def side_arrival(s, dst, sems, g, at):
        return pltpu.make_async_remote_copy(
            src_ref=dst.at[s, :, at, lanes_of(g)], dst_ref=dst.at[s, :, at, lanes_of(g)],
            send_sem=sems.at[0, s, g], recv_sem=sems.at[1, s, g],
            device_id={"cols": side_col(s)}, device_id_type=MESH,
        )

    mid_at, corner_at, all_at = pl.ds(CORNER, mid), pl.ds(0, CORNER), pl.ds(0, CORNER + mid)

    def mid_copy(s, g):
        return side_copy(s, own_side, side, mid_sems, g, mid_at)

    def corner_copy(s, g):
        return side_copy(s, own_side, side, corner_sems, g, corner_at)

    def srim_copy(s, g):
        return side_copy(s, srim_out, srim_in, srim_sems, g, all_at)

    for g in range(chunks):
        for way in ways:
            guarded(row_there(way), lambda way=way, g=g: halo_copy(way, g).start())
        for s in range(sides):
            guarded(side_there(s), lambda s=s, g=g: mid_copy(s, g).start())

    for way in ways:
        def clear(way=way):
            i = 0 if way < 0 else 1
            at = 0 if way < 0 else edge + tokens
            main[:, at : at + edge] = jnp.zeros((2, edge, width), BF16)
            rim_in[i] = jnp.zeros(rim_in.shape[1:], BF16)
        pl.when(jnp.logical_not(row_there(way)))(clear)
    for s in range(sides):
        if sides == 2:
            def clear_side(s=s):
                side[s] = jnp.zeros(side.shape[1:], BF16)
                srim_in[s] = jnp.zeros(srim_in.shape[1:], BF16)
            pl.when(jnp.logical_not(side_there(s)))(clear_side)

    for k in range(2):
        main[k, edge : edge + tokens] = kv_ref[k]

    d_att[...] = mm(og_ref[...], w_ref[...], 1, 1).astype(BF16)
    acc[...] = jnp.zeros(acc.shape, F32)
    sacc[...] = jnp.zeros(sacc.shape, F32)

    def put_bias(b, at, rows, cols, n):
        lane = lax.broadcasted_iota(jnp.int32, (n, step), 1)
        q_row = r * tile_h + b * QB + lane // tile_w
        q_col = c * tile_w + lane % tile_w
        first_r = jnp.clip(q_row - RAD, 0, image_h - WIN)
        first_c = jnp.clip(q_col - RAD, 0, image_w - WIN)
        ok = (rows >= first_r) & (rows < first_r + WIN) & (cols >= first_c) & (cols < first_c + WIN)
        bias[b, at : at + n] = jnp.where(ok, 0.0, -1e30)

    def near(b):
        return 0 if b == 0 else CORNER - NEAR

    for b in range(blocks):
        token = lax.broadcasted_iota(jnp.int32, (span, step), 0)
        put_bias(b, 0, r * tile_h + b * QB - RAD + token // tile_w, c * tile_w + token % tile_w, span)
        for s in range(sides):
            if sides == 1:
                first = c * tile_w + jnp.where(c == 0, tile_w, -RAD)
            else:
                first = c * tile_w + (tile_w if s else -RAD)
            at = span + s * sspan
            token = lax.broadcasted_iota(jnp.int32, (NEAR, step), 0) + near(b)
            lower = token >= RAD * RAD
            cell = jnp.where(lower, token - RAD * RAD, token)
            row = (cell * 10923) >> 16
            place = jnp.where(token < 2 * RAD * RAD, row + jnp.where(lower, tile_h, -RAD), 2 * image_h)
            put_bias(b, at, r * tile_h + place, first + cell - row * RAD, NEAR)
            token = lax.broadcasted_iota(jnp.int32, (mid, step), 0)
            row = (token * 10923) >> 16
            put_bias(b, at + NEAR, r * tile_h + row, first + token - row * RAD, mid)

    def lanes(p):
        return pl.ds(pl.multiple_of(p * PAIR, PAIR), PAIR)

    def keys_of(k, b, p):
        parts = [main[k, step * b : step * b + span, lanes(p)]]
        for s in range(sides):
            parts.append(side[s, k, near(b) : near(b) + NEAR, lanes(p)])
            parts.append(side[s, k, CORNER : CORNER + mid, lanes(p)])
        return jnp.concatenate(parts, axis=0)

    def split_heads(x):
        low_head = lax.broadcasted_iota(jnp.int32, x.shape, 1) < HD
        wide = x.astype(F32)
        return jnp.concatenate(
            [jnp.where(low_head, wide, 0.0), jnp.where(low_head, 0.0, wide)], axis=0
        ).astype(BF16)

    def queries_of(b, p):
        return split_heads(q_ref[step * b : step * (b + 1), lanes(p)].astype(F32) * scale)

    def own_heads(x):
        return jnp.concatenate([x[:HD, :step], x[HD:, step:]], axis=0)

    def attend(p, carry):
        for b in range(blocks):
            here = slice(step * b, step * (b + 1))
            keys, values = keys_of(0, b, p), keys_of(1, b, p)
            q_two = queries_of(b, p)
            d_blk = d_att[here, lanes(p)]
            d_two = split_heads(d_blk)
            hidden = bias[b]
            scores = mm(keys, q_two, 1, 1) + jnp.concatenate([hidden, hidden], axis=1)
            expd = jnp.exp(scores - jnp.max(scores, axis=0, keepdims=True))
            full = expd * (1.0 / jnp.sum(expd, axis=0, keepdims=True))
            low = full.astype(BF16)
            att = own_heads(mm(values, low, 0, 0)).astype(BF16)
            att_t[lanes(p), here] = att
            both = d_blk.astype(F32).T * att.astype(F32)
            delta = jnp.concatenate(
                [
                    jnp.sum(both[:HD], axis=0, keepdims=True),
                    jnp.sum(both[HD:], axis=0, keepdims=True),
                ],
                axis=1,
            )
            dscores = (full * (mm(values, d_two, 1, 1) - delta)).astype(BF16)
            dq = own_heads(mm(keys, dscores, 0, 0)) * scale
            dq_ref[here, lanes(p)] = dq.T.astype(BF16)
            for k, grad in ((0, mm(dscores, q_two, 1, 0)), (1, mm(low, d_two, 1, 0))):
                acc[k, step * b : step * b + span, lanes(p)] += grad[:span]
                for s in range(sides):
                    at = span + s * sspan
                    sacc[s, k, near(b) : near(b) + NEAR, lanes(p)] += grad[at : at + NEAR]
                    sacc[s, k, CORNER : CORNER + mid, lanes(p)] += grad[at + NEAR : at + sspan]
        return carry

    block_c = slab.shape[3]
    rows_c = width // n_rows
    bits = n_rows.bit_length() - 1
    order = [*range(1, bits), 0]
    og = og_ref[...]

    def dp_copy(k, g):
        to = lax.rem(d + k, n_dp)
        at = lanes_of(g)
        return pltpu.make_async_remote_copy(
            src_ref=slab_low.at[to, :, at], dst_ref=got_dp.at[k - 1, :, at],
            send_sem=dp_sems.at[0, k - 1, g], recv_sem=dp_sems.at[1, k - 1, g],
            device_id={"dp": to}, device_id_type=MESH,
        )

    def product(g):
        at = slice(g * part, (g + 1) * part)
        left = att_t[at]
        for j in range(n_cols):
            for e in range(n_dp):
                first = (j * n_dp + e) * block_c
                term = mm(left, og[:, first : first + block_c], 1, 0)
                slab[e, j, at] = term
                slab_low[e, j, at] = term.astype(BF16)
        for k in range(1, n_dp):
            dp_copy(k, g).start()

    def units(g):
        return range(g * part // rows_c, (g + 1) * part // rows_c)

    def bit_of(x, b):
        return lax.rem(x // 2**b, 2)

    def holds(u, level):
        ok = None
        for b in order[:level]:
            same = bit_of(r, b) == (u >> b) % 2
            ok = same if ok is None else ok & same
        return ok

    def both_of(a, b):
        return b if a is None else a & b

    def rows_copy(u, level):
        b = order[level]
        at = pl.ds(u * rows_c, rows_c)
        return pltpu.make_async_remote_copy(
            src_ref=low_rows.at[:, at], dst_ref=got_rows.at[level, :, at],
            send_sem=rows_sems.at[0, u], recv_sem=rows_sems.at[1 + level, u],
            device_id={"rows": r + (2**b if (u >> b) % 2 else -(2**b))}, device_id_type=MESH,
        )

    def rows_arrival(u, level):
        b = order[level]
        at = pl.ds(u * rows_c, rows_c)
        return pltpu.make_async_remote_copy(
            src_ref=low_rows.at[:, at], dst_ref=got_rows.at[level, :, at],
            send_sem=rows_sems.at[0, u], recv_sem=rows_sems.at[1 + level, u],
            device_id={"rows": r + (-(2**b) if (u >> b) % 2 else 2**b)}, device_id_type=MESH,
        )

    def pass_on(u, level, total):
        at = slice(u * rows_c, (u + 1) * rows_c)
        if level < bits:
            differs = bit_of(r, order[level]) != (u >> order[level]) % 2

            def send():
                for j in range(n_cols):
                    low_rows[j, at] = total[j].astype(BF16)
                rows_copy(u, level).start()

            guarded(differs, send)
            for j in range(n_cols):
                slab[d, j, at] = total[j]
        else:
            for j in range(n_cols):
                slab[d, j, at] = total[j]
                low_rows[j, at] = total[j].astype(BF16)
            for k in range(1, n_cols):
                cols_copy(k, u).start()

    def cols_copy(k, u):
        to = lax.rem(c + k, n_cols)
        return pltpu.make_async_remote_copy(
            src_ref=low_rows.at[to, pl.ds(u * rows_c, rows_c)], dst_ref=got_cols.at[k - 1],
            send_sem=cols_sems.at[0, k - 1], recv_sem=cols_sems.at[1, k - 1],
            device_id={"cols": to}, device_id_type=MESH,
        )

    def sum_dp(g):
        for k in range(1, n_dp):
            dp_copy(k, g).wait()
        for u in units(g):
            at = slice(u * rows_c, (u + 1) * rows_c)
            total = []
            for j in range(n_cols):
                term = slab[d, j, at]
                for k in range(1, n_dp):
                    term = term + got_dp[k - 1, j, at].astype(F32)
                total.append(term)
            pass_on(u, 0, total)

    def sum_rows(g, level):
        for u in units(g):
            at = slice(u * rows_c, (u + 1) * rows_c)

            def receive(u=u, at=at):
                rows_arrival(u, level).wait_recv()
                total = [slab[d, j, at] + got_rows[level, j, at].astype(F32) for j in range(n_cols)]
                pass_on(u, level + 1, total)

            guarded(holds(u, level + 1), receive)

    def wg_step(n):
        for level in range(bits, -1, -1):
            g = n - level
            if 0 <= g < chunks:
                if level == 0:
                    sum_dp(g)
                else:
                    sum_rows(g, level - 1)

    def send_corners(g):
        at = lanes_of(g)
        for way in ways:
            guarded(row_there(way), lambda way=way: halo_arrival(way, g).wait_recv())
        for s in range(sides):
            for k in range(2):
                both = jnp.concatenate([main[k, :edge, at], main[k, edge + tokens :, at]], axis=0)
                own_side[s, k, :CORNER, at] = mm(pick_rim[s], both, 1, 0).astype(BF16)
            guarded(side_there(s), lambda s=s: corner_copy(s, g).start())

    def wait_sides(g):
        for s in range(sides):
            def arrived(s=s):
                side_arrival(s, side, mid_sems, g, mid_at).wait_recv()
                side_arrival(s, side, corner_sems, g, corner_at).wait_recv()
            guarded(side_there(s), arrived)

    def send_srims(g):
        at = lanes_of(g)
        for s in range(sides):
            for k in range(2):
                srim_out[s, k, :, at] = sacc[s, k, :, at].astype(BF16)
            guarded(side_there(s), lambda s=s: srim_copy(s, g).start())

    def send_rims(g):
        at = lanes_of(g)
        for s in range(sides):
            guarded(side_there(s), lambda s=s: side_arrival(s, srim_in, srim_sems, g, all_at).wait_recv())
        for k in range(2):
            top, low = acc[k, :edge, at], acc[k, edge + tokens :, at]
            own = acc[k, edge : edge + tokens, at]
            for s in range(sides):
                both = mm(put_rim[s], srim_in[s, k, :CORNER, at], 1, 0)
                top, low = top + both[:edge], low + both[edge:]
                own = own + mm(put_own[s], srim_in[s, k, CORNER:, at], 1, 0)
            rim_out[0, k, :, at] = top.astype(BF16)
            rim_out[1, k, :, at] = low.astype(BF16)
            acc[k, edge : edge + tokens, at] = own
        for way in ways:
            guarded(row_there(way), lambda way=way: rim_copy(way, g).start())

    def finish(g):
        at = lanes_of(g)
        for way in ways:
            guarded(row_there(way), lambda way=way: rim_arrival(way, g).wait_recv())
        for k in range(2):
            acc[k, edge : 2 * edge, at] += rim_in[0, k, :, at].astype(F32)
            acc[k, tokens : edge + tokens, at] += rim_in[1, k, :, at].astype(F32)
            kvg_ref[k, :, at] = acc[k, edge : edge + tokens, at].astype(BF16)

    AHEAD = 2
    for g in range(AHEAD):
        send_corners(g)
    for g in range(chunks):
        if g + AHEAD < chunks:
            send_corners(g + AHEAD)
        wait_sides(g)
        lax.fori_loop(g * CHUNK, (g + 1) * CHUNK, attend, 0)
        send_srims(g)
        product(g)
        wg_step(g - 1)
        if g >= 1:
            send_rims(g - 1)
        if g >= 3:
            finish(g - 3)
    out_ref[...] = mm(att_t[...], w_ref[...], 0, 0).astype(BF16)
    wg_step(chunks - 1)
    send_rims(chunks - 1)
    for g in range(max(0, chunks - 3), chunks):
        wg_step(g + 3)
        finish(g)
    for n in range(chunks + 3, chunks + bits + 1):
        wg_step(n)

    for g in range(chunks):
        for way in ways:
            def sent(way=way, g=g):
                halo_copy(way, g).wait_send()
                rim_copy(way, g).wait_send()
            guarded(row_there(way), sent)
        for s in range(sides):
            def side_sent(s=s, g=g):
                mid_copy(s, g).wait_send()
                corner_copy(s, g).wait_send()
                srim_copy(s, g).wait_send()
            guarded(side_there(s), side_sent)
    for u in range(n_rows):
        for level in range(bits):
            differs = bit_of(r, order[level]) != (u >> order[level]) % 2
            guarded(both_of(holds(u, level), differs), lambda u=u, level=level: rows_copy(u, level).wait_send())
    total = slab[d, c, pl.ds(pl.multiple_of(r * rows_c, rows_c), rows_c)]
    for k in range(1, n_cols):
        cols_copy(k, r).wait()
        total = total + got_cols[k - 1].astype(F32)
    wg_ref[...] = total * (1.0 / math.sqrt(image_h * image_w * n_dp))


def local(n_rows, n_cols, n_dp, queries, keys_values, out_weight, out_grad):
    tile_h, tile_w, width = queries.shape[1:]
    tokens = tile_h * tile_w
    sides = 1 if n_cols == 2 else 2
    blocks = tile_h // QB
    pairs = width // PAIR
    edge = RAD * tile_w
    grown = tokens + 2 * edge
    mid = tile_h * RAD
    seen = (QB + 2 * RAD) * tile_w + sides * (NEAR + mid)
    step = QB * tile_w
    block_c = width // (n_cols * n_dp)
    rows_c = width // n_rows
    bits = n_rows.bit_length() - 1
    chunks = pairs // CHUNK
    vmem = pl.BlockSpec(memory_space=pltpu.VMEM)
    dma = pltpu.SemaphoreType.DMA
    out, dq, kvg, wg = pl.pallas_call(
        functools.partial(kernel, tile_h, tile_w, n_rows, n_cols, n_dp),
        out_shape=(
            jax.ShapeDtypeStruct((tokens, width), BF16),
            jax.ShapeDtypeStruct((tokens, width), BF16),
            jax.ShapeDtypeStruct((2, tokens, width), BF16),
            jax.ShapeDtypeStruct((rows_c, block_c), F32),
        ),
        in_specs=[vmem] * 4,
        out_specs=(vmem,) * 4,
        scratch_shapes=[
            pltpu.VMEM((2, grown, width), BF16),
            pltpu.VMEM((sides, 2, CORNER + mid, width), BF16),
            pltpu.VMEM((sides, 2, CORNER + mid, width), BF16),
            pltpu.VMEM((2, grown, width), F32),
            pltpu.VMEM((sides, 2, CORNER + mid, width), F32),
            pltpu.VMEM((blocks, seen, step), F32),
            pltpu.VMEM((width, tokens), BF16),
            pltpu.VMEM((tokens, width), BF16),
            pltpu.VMEM((2, 2, edge, width), BF16),
            pltpu.VMEM((2, 2, edge, width), BF16),
            pltpu.VMEM((sides, 2, CORNER + mid, width), BF16),
            pltpu.VMEM((sides, 2, CORNER + mid, width), BF16),
            pltpu.VMEM((n_dp, n_cols, width, block_c), F32),
            pltpu.VMEM((n_dp, n_cols, width, block_c), BF16),
            pltpu.VMEM((n_dp - 1, n_cols, width, block_c), BF16),
            pltpu.VMEM((n_cols, width, block_c), BF16),
            pltpu.VMEM((bits, n_cols, width, block_c), BF16),
            pltpu.VMEM((n_cols - 1, rows_c, block_c), BF16),
            dma((2, 2, chunks)), dma((2, sides, chunks)), dma((2, sides, chunks)),
            dma((2, 2, chunks)), dma((2, sides, chunks)),
            dma((2, n_dp - 1, chunks)), dma((1 + bits, n_rows)), dma((2, n_cols - 1)),
        ],
        compiler_params=pltpu.CompilerParams(
            collective_id=0, has_side_effects=True, vmem_limit_bytes=60 * 2**20
        ),
    )(
        queries.reshape(tokens, width),
        keys_values.reshape(2, tokens, width),
        out_weight,
        out_grad.reshape(tokens, width),
    )
    return (
        out.reshape(queries.shape),
        dq.reshape(queries.shape),
        kvg.reshape(keys_values.shape),
        wg,
    )


def solution(mesh):
    in_specs = (
        P("dp", "rows", "cols", None),
        P(None, "dp", "rows", "cols", None),
        P(),
        P("dp", "rows", "cols", None),
    )
    out_specs = (
        P("dp", "rows", "cols", None),
        P("dp", "rows", "cols", None),
        P(None, "dp", "rows", "cols", None),
        P("rows", ("cols", "dp")),
    )
    sizes = (mesh.shape["rows"], mesh.shape["cols"], mesh.shape["dp"])
    return jax.shard_map(
        functools.partial(local, *sizes),
        mesh=mesh, in_specs=in_specs, out_specs=out_specs, check_vma=False,
    )
```

```python
import functools
import math

import jax
import jax.numpy as jnp
from jax import lax
from jax.experimental import pallas as pl
from jax.experimental.pallas import tpu as pltpu
from jax.sharding import PartitionSpec as P

NH = 16
HD = 64
RAD = 6
WIN = 13
QB = 8
PAIR = 2 * HD
CHUNK = 1
CORNER = -(-RAD * RAD // 16) * 16
AHEAD = 5
WINDOW = 8
HOLD = 4
RATE = 1
WG_TAIL = 3
LAGS = (3, 7, 11, 15)
MESH = pl.DeviceIdType.MESH
F32 = jnp.float32
BF16 = jnp.bfloat16


def mm(a, b, ca, cb):
    return lax.dot_general(a, b, (((ca,), (cb,)), ((), ())), preferred_element_type=F32)


def kernel(
    tile_h, tile_w, n_rows, n_cols, n_dp,
    q_ref, kv_ref, w_ref, og_ref,
    out_ref, dq_ref, kvg_ref, wg_ref,
    main, corner, own_corner, mid, own_mid, acc, macc, bias, att_t, d_att,
    rim_out, rim_in, crim_out, crim_in, mrim_out, mrim_in,
    slab, slab_low, got_dp, low_rows, got_rows, got_cols,
    halo_sems, mid_sems, corner_sems, rim_sems, crim_sems, mrim_sems, dp_sems, rows_sems, cols_sems,
):
    sides = mid.shape[0]
    blocks = tile_h // QB
    tokens = tile_h * tile_w
    width = q_ref.shape[1]
    pairs = width // PAIR
    edge = RAD * tile_w
    span = (QB + 2 * RAD) * tile_w
    strip = tile_h * RAD
    sspan = CORNER + strip
    step = QB * tile_w
    image_h, image_w = tile_h * n_rows, tile_w * n_cols
    scale = 1.0 / math.sqrt(HD)
    r, c, d = lax.axis_index("rows"), lax.axis_index("cols"), lax.axis_index("dp")
    chunks = pairs // CHUNK
    turn = [g for h in range(2) for g in (h, chunks - 2 + h, 2 + h, chunks - 4 + h)] if chunks == 8 else [*range(chunks)]
    part = CHUNK * PAIR
    first_b = lax.rem(r, 2)
    phases = (first_b, 1 - first_b)

    def lanes_of(g):
        return pl.ds(g * part, part)

    def row_there(b):
        return (r + 2 * b > 0) & (r + 2 * b < n_rows + 1)

    def side_there(s):
        if sides == 1:
            return None
        return c > 0 if s == 0 else c < n_cols - 1

    def guarded(ok, action):
        if ok is None:
            action()
        else:
            pl.when(ok)(action)

    def side_col(s):
        return 1 - c if sides == 1 else c + (2 * s - 1)

    def slot(s):
        return 0 if sides == 1 else 1 - s

    def starts_at(s):
        if sides == 1:
            return (1 - c) * (tile_w - RAD)
        return 0 if s == 0 else tile_w - RAD

    barrier = pltpu.get_barrier_semaphore()
    for k in range(1, n_rows):
        pl.semaphore_signal(barrier, 1, device_id={"rows": lax.rem(r + k, n_rows)}, device_id_type=MESH)
    for k in range(1, n_cols):
        pl.semaphore_signal(barrier, 1, device_id={"cols": lax.rem(c + k, n_cols)}, device_id_type=MESH)
    for k in range(1, n_dp):
        pl.semaphore_signal(barrier, 1, device_id={"dp": lax.rem(d + k, n_dp)}, device_id_type=MESH)

    def place(token, s):
        row = (token * 10923) >> 16
        return row * tile_w + token - row * RAD + starts_at(s)

    def one_hot(n, cells, used, s, token_axis):
        shape = (n, cells) if token_axis == 0 else (cells, n)
        token = lax.broadcasted_iota(jnp.int32, shape, token_axis)
        cell = lax.broadcasted_iota(jnp.int32, shape, 1 - token_axis)
        return ((place(token, s) == cell) & (token < used)).astype(F32).astype(BF16)

    pick_corner = [one_hot(CORNER, edge, RAD * RAD, s, 0) for s in range(sides)]
    put_corner = [one_hot(CORNER, edge, RAD * RAD, s, 1) for s in range(sides)]
    put_mid = [one_hot(strip, tokens, strip, s, 1) for s in range(sides)]
    for s in range(sides):
        chosen = one_hot(strip, tokens, strip, s, 0)
        for k in range(2):
            own_mid[s, k] = mm(chosen, kv_ref[k], 1, 0).astype(BF16)

    pl.semaphore_wait(barrier, n_rows + n_cols + n_dp - 3)

    def row_link(b, src, dst, sems, g):
        return pltpu.make_async_remote_copy(
            src_ref=src, dst_ref=dst, send_sem=sems.at[0, b, g], recv_sem=sems.at[1, 1 - b, g],
            device_id={"rows": r + 2 * b - 1}, device_id_type=MESH,
        )

    def row_arrival(b, dst, sems, g):
        return pltpu.make_async_remote_copy(
            src_ref=dst, dst_ref=dst, send_sem=sems.at[0, b, g], recv_sem=sems.at[1, b, g],
            device_id={"rows": r + 2 * b - 1}, device_id_type=MESH,
        )

    def halo_rows(b):
        return pl.ds(pl.multiple_of(b * (edge + tokens), 16), edge)

    def halo_place(b, g):
        return main.at[:, halo_rows(b), lanes_of(g)]

    def halo_copy(b, g):
        own = kv_ref.at[:, pl.ds(pl.multiple_of(b * (tokens - edge), 16), edge), lanes_of(g)]
        return row_link(b, own, halo_place(1 - b, g), halo_sems, g)

    def halo_arrival(b, g):
        return row_arrival(b, halo_place(b, g), halo_sems, g)

    def rim_copy(b, g):
        at = lanes_of(g)
        return row_link(b, rim_out.at[b, :, :, at], rim_in.at[1 - b, :, :, at], rim_sems, g)

    def rim_arrival(b, g):
        return row_arrival(b, rim_in.at[b, :, :, lanes_of(g)], rim_sems, g)

    def side_copy(s, src, dst, send, recv):
        return pltpu.make_async_remote_copy(
            src_ref=src, dst_ref=dst, send_sem=send, recv_sem=recv,
            device_id={"cols": side_col(s)}, device_id_type=MESH,
        )

    def mid_copy(s, g, src=own_mid, dst=mid, sems=mid_sems):
        at, far = lanes_of(g), slot(s)
        return side_copy(s, src.at[s, :, :, at], dst.at[far, :, :, at], sems.at[0, s, g], sems.at[1, far, g])

    def mid_arrival(s, g, dst=mid, sems=mid_sems):
        at = dst.at[s, :, :, lanes_of(g)]
        return side_copy(s, at, at, sems.at[0, s, g], sems.at[1, s, g])

    def corner_copy(s, b, g, src=own_corner, dst=corner, sems=corner_sems):
        at, far = lanes_of(g), slot(s)
        return side_copy(
            s, src.at[s, b, :, :, at], dst.at[far, b, :, :, at], sems.at[0, s, b, g], sems.at[1, far, b, g]
        )

    def corner_arrival(s, b, g, dst=corner, sems=corner_sems):
        at = dst.at[s, b, :, :, lanes_of(g)]
        return side_copy(s, at, at, sems.at[0, s, b, g], sems.at[1, s, b, g])

    def mrim_copy(s, g):
        return mid_copy(s, g, mrim_out, mrim_in, mrim_sems)

    def mrim_arrival(s, g):
        return mid_arrival(s, g, mrim_in, mrim_sems)

    def crim_copy(s, b, g):
        return corner_copy(s, b, g, crim_out, crim_in, crim_sems)

    def crim_arrival(s, b, g):
        return corner_arrival(s, b, g, crim_in, crim_sems)

    def send_halo(i):
        if i < 2 * chunks:
            b, g = phases[i // chunks], turn[i % chunks]
            pl.when(row_there(b))(halo_copy(b, g).start)
        if i < chunks:
            for s in range(sides):
                guarded(side_there(s), mid_copy(s, turn[i]).start)

    for i in range(WINDOW):
        send_halo(i)

    for b in range(2):
        def clear(b=b):
            at = b * (edge + tokens)
            main[:, at : at + edge] = jnp.zeros((2, edge, width), BF16)
            rim_in[b] = jnp.zeros(rim_in.shape[1:], BF16)
        pl.when(jnp.logical_not(row_there(b)))(clear)
    for s in range(sides):
        if sides == 2:
            def clear_side(s=s):
                for ref in (mid, corner, crim_in, mrim_in):
                    ref[s] = jnp.zeros(ref.shape[1:], BF16)
            pl.when(jnp.logical_not(side_there(s)))(clear_side)

    for k in range(2):
        main[k, edge : edge + tokens] = kv_ref[k]

    d_att[...] = mm(og_ref[...], w_ref[...], 1, 1).astype(BF16)
    acc[...] = jnp.zeros(acc.shape, F32)

    def put_bias(b, at, rows, cols, n):
        lane = lax.broadcasted_iota(jnp.int32, (n, step), 1)
        q_row = r * tile_h + b * QB + lane // tile_w
        q_col = c * tile_w + lane % tile_w
        first_r = jnp.clip(q_row - RAD, 0, image_h - WIN)
        first_c = jnp.clip(q_col - RAD, 0, image_w - WIN)
        ok = (rows >= first_r) & (rows < first_r + WIN) & (cols >= first_c) & (cols < first_c + WIN)
        bias[b, at : at + n] = jnp.where(ok, 0.0, -1e30)

    for b in range(blocks):
        token = lax.broadcasted_iota(jnp.int32, (span, step), 0)
        put_bias(b, 0, r * tile_h + b * QB - RAD + token // tile_w, c * tile_w + token % tile_w, span)
        for s in range(sides):
            if sides == 1:
                first = c * tile_w + jnp.where(c == 0, tile_w, -RAD)
            else:
                first = c * tile_w + (tile_w if s else -RAD)
            at = span + s * sspan
            token = lax.broadcasted_iota(jnp.int32, (CORNER, step), 0)
            row = (token * 10923) >> 16
            tall = jnp.where(token < RAD * RAD, row + (tile_h if b else -RAD), 2 * image_h)
            put_bias(b, at, r * tile_h + tall, first + token - row * RAD, CORNER)
            token = lax.broadcasted_iota(jnp.int32, (strip, step), 0)
            row = (token * 10923) >> 16
            put_bias(b, at + CORNER, r * tile_h + row, first + token - row * RAD, strip)

    def lanes(p):
        return pl.ds(pl.multiple_of(p * PAIR, PAIR), PAIR)

    def block_rows(b):
        return pl.ds(pl.multiple_of(b * step, step), span)

    def keys_of(k, b, p):
        parts = [main[k, block_rows(b), lanes(p)]]
        for s in range(sides):
            parts.append(corner[s, b, k, :, lanes(p)])
            parts.append(mid[s, k, :, lanes(p)])
        return jnp.concatenate(parts, axis=0)

    def split_heads(x):
        low_head = lax.broadcasted_iota(jnp.int32, x.shape, 1) < HD
        wide = x.astype(F32)
        return jnp.concatenate(
            [jnp.where(low_head, wide, 0.0), jnp.where(low_head, 0.0, wide)], axis=0
        ).astype(BF16)

    def queries_of(here, p):
        return split_heads(q_ref[here, lanes(p)].astype(F32) * scale)

    def own_heads(x):
        return jnp.concatenate([x[:HD, :step], x[HD:, step:]], axis=0)

    def attend(n, p):
        b = phases[n]
        here = pl.ds(pl.multiple_of(b * step, step), step)
        keys, values = keys_of(0, b, p), keys_of(1, b, p)
        q_two = queries_of(here, p)
        d_blk = d_att[here, lanes(p)]
        d_two = split_heads(d_blk)
        hidden = bias[b]
        scores = mm(keys, q_two, 1, 1) + jnp.concatenate([hidden, hidden], axis=1)
        expd = jnp.exp(scores - jnp.max(scores, axis=0, keepdims=True))
        full = expd * (1.0 / jnp.sum(expd, axis=0, keepdims=True))
        low = full.astype(BF16)
        att = own_heads(mm(values, low, 0, 0)).astype(BF16)
        att_t[lanes(p), here] = att
        both = d_blk.astype(F32).T * att.astype(F32)
        delta = jnp.concatenate(
            [
                jnp.sum(both[:HD], axis=0, keepdims=True),
                jnp.sum(both[HD:], axis=0, keepdims=True),
            ],
            axis=1,
        )
        dscores = (full * (mm(values, d_two, 1, 1) - delta)).astype(BF16)
        dq = own_heads(mm(keys, dscores, 0, 0)) * scale
        dq_ref[here, lanes(p)] = dq.T.astype(BF16)
        for k, grad in ((0, mm(dscores, q_two, 1, 0)), (1, mm(low, d_two, 1, 0))):
            acc[k, block_rows(b), lanes(p)] += grad[:span]
            for s in range(sides):
                at = span + s * sspan
                crim_out[s, b, k, :, lanes(p)] = grad[at : at + CORNER].astype(BF16)
                rest = grad[at + CORNER : at + sspan]
                if n == 0:
                    macc[s, k, :, lanes(p)] = rest
                else:
                    mrim_out[s, k, :, lanes(p)] = (macc[s, k, :, lanes(p)] + rest).astype(BF16)

    block_c = slab.shape[3]
    rows_c = width // n_rows
    bits = n_rows.bit_length() - 1
    order = [*range(1, bits), 0]
    og = og_ref[...]

    def dp_copy(k, g):
        to = lax.rem(d + k, n_dp)
        at = lanes_of(g)
        return pltpu.make_async_remote_copy(
            src_ref=slab_low.at[to, :, at], dst_ref=got_dp.at[k - 1, :, at],
            send_sem=dp_sems.at[0, k - 1, g], recv_sem=dp_sems.at[1, k - 1, g],
            device_id={"dp": to}, device_id_type=MESH,
        )

    def product(g):
        at = slice(g * part, (g + 1) * part)
        left = att_t[at]
        for j in range(n_cols):
            for e in range(n_dp):
                first = (j * n_dp + e) * block_c
                term = mm(left, og[:, first : first + block_c], 1, 0)
                slab[e, j, at] = term
                slab_low[e, j, at] = term.astype(BF16)
        for k in range(1, n_dp):
            dp_copy(k, g).start()

    def units(g):
        return range(g * part // rows_c, (g + 1) * part // rows_c)

    def bit_of(x, b):
        return lax.rem(x // 2**b, 2)

    def holds(u, level):
        ok = None
        for b in order[:level]:
            same = bit_of(r, b) == (u >> b) % 2
            ok = same if ok is None else ok & same
        return ok

    def both_of(a, b):
        return b if a is None else a & b

    def rows_copy(u, level):
        b = order[level]
        at = pl.ds(u * rows_c, rows_c)
        return pltpu.make_async_remote_copy(
            src_ref=low_rows.at[:, at], dst_ref=got_rows.at[level, :, at],
            send_sem=rows_sems.at[0, u], recv_sem=rows_sems.at[1 + level, u],
            device_id={"rows": r + (2**b if (u >> b) % 2 else -(2**b))}, device_id_type=MESH,
        )

    def rows_arrival(u, level):
        b = order[level]
        at = pl.ds(u * rows_c, rows_c)
        return pltpu.make_async_remote_copy(
            src_ref=low_rows.at[:, at], dst_ref=got_rows.at[level, :, at],
            send_sem=rows_sems.at[0, u], recv_sem=rows_sems.at[1 + level, u],
            device_id={"rows": r + (-(2**b) if (u >> b) % 2 else 2**b)}, device_id_type=MESH,
        )

    def pass_on(u, level, total):
        at = slice(u * rows_c, (u + 1) * rows_c)
        if level < bits:
            differs = bit_of(r, order[level]) != (u >> order[level]) % 2

            def send():
                for j in range(n_cols):
                    low_rows[j, at] = total[j].astype(BF16)
                rows_copy(u, level).start()

            guarded(differs, send)
            for j in range(n_cols):
                slab[d, j, at] = total[j]
        else:
            for j in range(n_cols):
                slab[d, j, at] = total[j]
                low_rows[j, at] = total[j].astype(BF16)
            for k in range(1, n_cols):
                cols_copy(k, u).start()

    def cols_copy(k, u):
        to = lax.rem(c + k, n_cols)
        return pltpu.make_async_remote_copy(
            src_ref=low_rows.at[to, pl.ds(u * rows_c, rows_c)], dst_ref=got_cols.at[k - 1],
            send_sem=cols_sems.at[0, k - 1], recv_sem=cols_sems.at[1, k - 1],
            device_id={"cols": to}, device_id_type=MESH,
        )

    def sum_dp(g):
        for k in range(1, n_dp):
            dp_copy(k, g).wait()
        for u in units(g):
            at = slice(u * rows_c, (u + 1) * rows_c)
            total = []
            for j in range(n_cols):
                term = slab[d, j, at]
                for k in range(1, n_dp):
                    term = term + got_dp[k - 1, j, at].astype(F32)
                total.append(term)
            pass_on(u, 0, total)

    def sum_rows(g, level):
        for u in units(g):
            at = slice(u * rows_c, (u + 1) * rows_c)

            def receive(u=u, at=at):
                rows_arrival(u, level).wait_recv()
                total = [slab[d, j, at] + got_rows[level, j, at].astype(F32) for j in range(n_cols)]
                pass_on(u, level + 1, total)

            guarded(holds(u, level + 1), receive)

    lags = LAGS + tuple(range(LAGS[-1] + 1, LAGS[-1] + 1 + bits - 3))

    def wg_step(n):
        for level in range(bits, -1, -1):
            i = n - lags[level]
            if 0 <= i < chunks:
                if level == 0:
                    sum_dp(turn[i])
                else:
                    sum_rows(turn[i], level - 1)

    def send_corners(n, i):
        b, g = phases[n], turn[i]
        at = lanes_of(g)
        pl.when(row_there(b))(lambda: halo_arrival(b, g).wait_recv())
        send_halo(n * chunks + i + WINDOW)
        for s in range(sides):
            for k in range(2):
                own_corner[s, b, k, :, at] = mm(pick_corner[s], main[k, halo_rows(b), at], 1, 0).astype(BF16)
            guarded(side_there(s), corner_copy(s, b, g).start)

    def wait_sides(n, g):
        for s in range(sides):
            def arrived(s=s):
                if n == 0:
                    mid_arrival(s, g).wait_recv()
                corner_arrival(s, phases[n], g).wait_recv()
            guarded(side_there(s), arrived)

    def send_sides(n, g):
        for s in range(sides):
            def send(s=s):
                crim_copy(s, phases[n], g).start()
                if n == 1:
                    mrim_copy(s, g).start()
            guarded(side_there(s), send)

    def send_rims(n, g):
        b, at = phases[n], lanes_of(g)
        for s in range(sides):
            guarded(side_there(s), lambda s=s: crim_arrival(s, b, g).wait_recv())
        for k in range(2):
            total = acc[k, halo_rows(b), at]
            for s in range(sides):
                total = total + mm(put_corner[s], crim_in[s, b, k, :, at], 1, 0)
            rim_out[b, k, :, at] = total.astype(BF16)
        pl.when(row_there(b))(rim_copy(b, g).start)

    def finish(g):
        at = lanes_of(g)
        for s in range(sides):
            guarded(side_there(s), lambda s=s: mrim_arrival(s, g).wait_recv())
        for b in range(2):
            pl.when(row_there(b))(lambda b=b: rim_arrival(b, g).wait_recv())
        for k in range(2):
            own = acc[k, edge : edge + tokens, at]
            for s in range(sides):
                own = own + mm(put_mid[s], mrim_in[s, k, :, at], 1, 0)
            kvg_ref[k, edge : tokens - edge, at] = own[edge : tokens - edge].astype(BF16)
            kvg_ref[k, :edge, at] = (own[:edge] + rim_in[0, k, :, at].astype(F32)).astype(BF16)
            kvg_ref[k, tokens - edge :, at] = (own[tokens - edge :] + rim_in[1, k, :, at].astype(F32)).astype(BF16)

    steps = 2 * chunks
    rims = [*range(steps)]

    def flush_rims(count):
        for _ in range(count):
            q = rims.pop(0)
            send_rims(q // chunks, turn[q % chunks])

    for q in range(AHEAD):
        send_corners(q // chunks, q % chunks)
    for q in range(steps):
        n, g = q // chunks, turn[q % chunks]
        if q + AHEAD < steps:
            send_corners((q + AHEAD) // chunks, (q + AHEAD) % chunks)
        wait_sides(n, g)
        attend(n, g)
        send_sides(n, g)
        if n == 1:
            product(g)
            wg_step(q - chunks)
        if q >= HOLD:
            flush_rims(RATE)
    n = chunks
    while rims or n < chunks + WG_TAIL:
        if n < chunks + WG_TAIL:
            wg_step(n)
            n += 1
        flush_rims(min(len(rims), RATE))
    out_ref[...] = mm(att_t[...], w_ref[...], 0, 0).astype(BF16)
    for i in range(chunks):
        if n < chunks + lags[bits]:
            wg_step(n)
            n += 1
        finish(turn[i])
    while n < chunks + lags[bits]:
        wg_step(n)
        n += 1

    for g in range(chunks):
        for b in range(2):
            def sent(b=b, g=g):
                halo_copy(b, g).wait_send()
                rim_copy(b, g).wait_send()
            pl.when(row_there(b))(sent)
        for s in range(sides):
            def side_sent(s=s, g=g):
                mid_copy(s, g).wait_send()
                mrim_copy(s, g).wait_send()
                for b in range(2):
                    corner_copy(s, b, g).wait_send()
                    crim_copy(s, b, g).wait_send()
            guarded(side_there(s), side_sent)
    for u in range(n_rows):
        for level in range(bits):
            differs = bit_of(r, order[level]) != (u >> order[level]) % 2
            guarded(both_of(holds(u, level), differs), lambda u=u, level=level: rows_copy(u, level).wait_send())
    total = slab[d, c, pl.ds(pl.multiple_of(r * rows_c, rows_c), rows_c)]
    for k in range(1, n_cols):
        cols_copy(k, r).wait()
        total = total + got_cols[k - 1].astype(F32)
    wg_ref[...] = total * (1.0 / math.sqrt(image_h * image_w * n_dp))


def local(n_rows, n_cols, n_dp, queries, keys_values, out_weight, out_grad):
    tile_h, tile_w, width = queries.shape[1:]
    tokens = tile_h * tile_w
    sides = 1 if n_cols == 2 else 2
    blocks = tile_h // QB
    pairs = width // PAIR
    edge = RAD * tile_w
    grown = tokens + 2 * edge
    strip = tile_h * RAD
    seen = (QB + 2 * RAD) * tile_w + sides * (CORNER + strip)
    step = QB * tile_w
    block_c = width // (n_cols * n_dp)
    rows_c = width // n_rows
    bits = n_rows.bit_length() - 1
    chunks = pairs // CHUNK
    vmem = pl.BlockSpec(memory_space=pltpu.VMEM)
    dma = pltpu.SemaphoreType.DMA
    shapes = (
        jax.ShapeDtypeStruct((tokens, width), BF16),
        jax.ShapeDtypeStruct((tokens, width), BF16),
        jax.ShapeDtypeStruct((2, tokens, width), BF16),
        jax.ShapeDtypeStruct((rows_c, block_c), F32),
    )
    results = pl.pallas_call(
        functools.partial(kernel, tile_h, tile_w, n_rows, n_cols, n_dp),
        out_shape=tuple(pltpu.VMEM(x.shape, x.dtype) for x in shapes),
        in_specs=[vmem] * 4,
        out_specs=(vmem,) * 4,
        scratch_shapes=[
            pltpu.VMEM((2, grown, width), BF16),
            pltpu.VMEM((sides, 2, 2, CORNER, width), BF16),
            pltpu.VMEM((sides, 2, 2, CORNER, width), BF16),
            pltpu.VMEM((sides, 2, strip, width), BF16),
            pltpu.VMEM((sides, 2, strip, width), BF16),
            pltpu.VMEM((2, grown, width), F32),
            pltpu.VMEM((sides, 2, strip, width), F32),
            pltpu.VMEM((blocks, seen, step), F32),
            pltpu.VMEM((width, tokens), BF16),
            pltpu.VMEM((tokens, width), BF16),
            pltpu.VMEM((2, 2, edge, width), BF16),
            pltpu.VMEM((2, 2, edge, width), BF16),
            pltpu.VMEM((sides, 2, 2, CORNER, width), BF16),
            pltpu.VMEM((sides, 2, 2, CORNER, width), BF16),
            pltpu.VMEM((sides, 2, strip, width), BF16),
            pltpu.VMEM((sides, 2, strip, width), BF16),
            pltpu.VMEM((n_dp, n_cols, width, block_c), F32),
            pltpu.VMEM((n_dp, n_cols, width, block_c), BF16),
            pltpu.VMEM((n_dp - 1, n_cols, width, block_c), BF16),
            pltpu.VMEM((n_cols, width, block_c), BF16),
            pltpu.VMEM((bits, n_cols, width, block_c), BF16),
            pltpu.VMEM((n_cols - 1, rows_c, block_c), BF16),
            dma((2, 2, chunks)), dma((2, sides, chunks)), dma((2, sides, 2, chunks)),
            dma((2, 2, chunks)), dma((2, sides, 2, chunks)), dma((2, sides, chunks)),
            dma((2, n_dp - 1, chunks)), dma((1 + bits, n_rows)), dma((2, n_cols - 1)),
        ],
        compiler_params=pltpu.CompilerParams(
            collective_id=0, has_side_effects=True, vmem_limit_bytes=60 * 2**20
        ),
    )(
        queries.reshape(tokens, width),
        keys_values.reshape(2, tokens, width),
        out_weight,
        out_grad.reshape(tokens, width),
    )
    out, dq, kvg, wg = results
    return (
        out.reshape(queries.shape),
        dq.reshape(queries.shape),
        kvg.reshape(keys_values.shape),
        wg,
    )


def solution(mesh):
    in_specs = (
        P("dp", "rows", "cols", None),
        P(None, "dp", "rows", "cols", None),
        P(),
        P("dp", "rows", "cols", None),
    )
    out_specs = (
        P("dp", "rows", "cols", None),
        P("dp", "rows", "cols", None),
        P(None, "dp", "rows", "cols", None),
        P("rows", ("cols", "dp")),
    )
    sizes = (mesh.shape["rows"], mesh.shape["cols"], mesh.shape["dp"])
    return jax.shard_map(
        functools.partial(local, *sizes),
        mesh=mesh, in_specs=in_specs, out_specs=out_specs, check_vma=False,
    )
```

```python
import functools
import math

import jax
import jax.numpy as jnp
from jax import lax
from jax.experimental import pallas as pl
from jax.experimental.pallas import tpu as pltpu
from jax.sharding import PartitionSpec as P

NH = 16
HD = 64
RAD = 6
WIN = 13
QB = 8
PAIR = 2 * HD
CHUNK = 1
CORNER = -(-RAD * RAD // 16) * 16
AHEAD = 6
WINDOW = 8
HOLD = 4
SHIFT = 6
RATE = 1
WG_TAIL = 3
LAGS = (3, 8)
MESH = pl.DeviceIdType.MESH
F32 = jnp.float32
BF16 = jnp.bfloat16


def mm(a, b, ca, cb):
    return lax.dot_general(a, b, (((ca,), (cb,)), ((), ())), preferred_element_type=F32)


def kernel(
    tile_h, tile_w, n_rows, n_cols, n_dp,
    q_ref, kv_ref, w_ref, og_ref,
    out_ref, dq_ref, kvg_ref, wg_ref,
    main, corner, own_corner, mid, own_mid, acc, macc, bias, att_t, d_att,
    rim_out, rim_in, crim_out, crim_in, mrim_out, mrim_in,
    slab, slab_low, got_dp, low_cols, got_cols, low_rows, got_rows,
    halo_sems, mid_sems, corner_sems, rim_sems, crim_sems, mrim_sems, dp_sems, cols_sems, rows_sems,
):
    sides = mid.shape[0]
    blocks = tile_h // QB
    tokens = tile_h * tile_w
    width = q_ref.shape[1]
    pairs = width // PAIR
    edge = RAD * tile_w
    span = (QB + 2 * RAD) * tile_w
    strip = tile_h * RAD
    sspan = CORNER + strip
    step = QB * tile_w
    image_h, image_w = tile_h * n_rows, tile_w * n_cols
    scale = 1.0 / math.sqrt(HD)
    r, c, d = lax.axis_index("rows"), lax.axis_index("cols"), lax.axis_index("dp")
    chunks = pairs // CHUNK
    turn = [g for h in range(2) for g in (h, chunks - 2 + h, 2 + h, chunks - 4 + h)] if chunks == 8 else [*range(chunks)]
    part = CHUNK * PAIR
    seq = [n * chunks + t - n * SHIFT for t in range(chunks + SHIFT) for n in range(2) if 0 <= t - n * SHIFT < chunks]
    first_b = lax.rem(r, 2)
    phases = (first_b, 1 - first_b)

    def lanes_of(g):
        return pl.ds(g * part, part)

    def row_there(b):
        return (r + 2 * b > 0) & (r + 2 * b < n_rows + 1)

    def side_there(s):
        if sides == 1:
            return None
        return c > 0 if s == 0 else c < n_cols - 1

    def guarded(ok, action):
        if ok is None:
            action()
        else:
            pl.when(ok)(action)

    def side_col(s):
        return 1 - c if sides == 1 else c + (2 * s - 1)

    def slot(s):
        return 0 if sides == 1 else 1 - s

    def starts_at(s):
        if sides == 1:
            return (1 - c) * (tile_w - RAD)
        return 0 if s == 0 else tile_w - RAD

    barrier = pltpu.get_barrier_semaphore()
    for k in range(1, n_rows):
        pl.semaphore_signal(barrier, 1, device_id={"rows": lax.rem(r + k, n_rows)}, device_id_type=MESH)
    for k in range(1, n_cols):
        pl.semaphore_signal(barrier, 1, device_id={"cols": lax.rem(c + k, n_cols)}, device_id_type=MESH)
    for k in range(1, n_dp):
        pl.semaphore_signal(barrier, 1, device_id={"dp": lax.rem(d + k, n_dp)}, device_id_type=MESH)

    def place(token, s):
        row = (token * 10923) >> 16
        return row * tile_w + token - row * RAD + starts_at(s)

    def one_hot(n, cells, used, s, token_axis):
        shape = (n, cells) if token_axis == 0 else (cells, n)
        token = lax.broadcasted_iota(jnp.int32, shape, token_axis)
        cell = lax.broadcasted_iota(jnp.int32, shape, 1 - token_axis)
        return ((place(token, s) == cell) & (token < used)).astype(F32).astype(BF16)

    pick_corner = [one_hot(CORNER, edge, RAD * RAD, s, 0) for s in range(sides)]
    put_corner = [one_hot(CORNER, edge, RAD * RAD, s, 1) for s in range(sides)]
    put_mid = [one_hot(strip, tokens, strip, s, 1) for s in range(sides)]
    for s in range(sides):
        chosen = one_hot(strip, tokens, strip, s, 0)
        for k in range(2):
            own_mid[s, k] = mm(chosen, kv_ref[k], 1, 0).astype(BF16)

    pl.semaphore_wait(barrier, n_rows + n_cols + n_dp - 3)

    def row_link(b, src, dst, sems, g):
        return pltpu.make_async_remote_copy(
            src_ref=src, dst_ref=dst, send_sem=sems.at[0, b, g], recv_sem=sems.at[1, 1 - b, g],
            device_id={"rows": r + 2 * b - 1}, device_id_type=MESH,
        )

    def row_arrival(b, dst, sems, g):
        return pltpu.make_async_remote_copy(
            src_ref=dst, dst_ref=dst, send_sem=sems.at[0, b, g], recv_sem=sems.at[1, b, g],
            device_id={"rows": r + 2 * b - 1}, device_id_type=MESH,
        )

    def halo_rows(b):
        return pl.ds(pl.multiple_of(b * (edge + tokens), 16), edge)

    def halo_place(b, g):
        return main.at[:, halo_rows(b), lanes_of(g)]

    def halo_copy(b, g):
        own = kv_ref.at[:, pl.ds(pl.multiple_of(b * (tokens - edge), 16), edge), lanes_of(g)]
        return row_link(b, own, halo_place(1 - b, g), halo_sems, g)

    def halo_arrival(b, g):
        return row_arrival(b, halo_place(b, g), halo_sems, g)

    def rim_copy(b, g):
        at = lanes_of(g)
        return row_link(b, rim_out.at[b, :, :, at], rim_in.at[1 - b, :, :, at], rim_sems, g)

    def rim_arrival(b, g):
        return row_arrival(b, rim_in.at[b, :, :, lanes_of(g)], rim_sems, g)

    def side_copy(s, src, dst, send, recv):
        return pltpu.make_async_remote_copy(
            src_ref=src, dst_ref=dst, send_sem=send, recv_sem=recv,
            device_id={"cols": side_col(s)}, device_id_type=MESH,
        )

    def mid_copy(s, g, src=own_mid, dst=mid, sems=mid_sems):
        at, far = lanes_of(g), slot(s)
        return side_copy(s, src.at[s, :, :, at], dst.at[far, :, :, at], sems.at[0, s, g], sems.at[1, far, g])

    def mid_arrival(s, g, dst=mid, sems=mid_sems):
        at = dst.at[s, :, :, lanes_of(g)]
        return side_copy(s, at, at, sems.at[0, s, g], sems.at[1, s, g])

    def corner_copy(s, b, g, src=own_corner, dst=corner, sems=corner_sems):
        at, far = lanes_of(g), slot(s)
        return side_copy(
            s, src.at[s, b, :, :, at], dst.at[far, b, :, :, at], sems.at[0, s, b, g], sems.at[1, far, b, g]
        )

    def corner_arrival(s, b, g, dst=corner, sems=corner_sems):
        at = dst.at[s, b, :, :, lanes_of(g)]
        return side_copy(s, at, at, sems.at[0, s, b, g], sems.at[1, s, b, g])

    def mrim_copy(s, g):
        return mid_copy(s, g, mrim_out, mrim_in, mrim_sems)

    def mrim_arrival(s, g):
        return mid_arrival(s, g, mrim_in, mrim_sems)

    def crim_copy(s, b, g):
        return corner_copy(s, b, g, crim_out, crim_in, crim_sems)

    def crim_arrival(s, b, g):
        return corner_arrival(s, b, g, crim_in, crim_sems)

    def send_halo(i):
        if i < 2 * chunks:
            q = seq[i]
            b, g = phases[q // chunks], turn[q % chunks]
            pl.when(row_there(b))(halo_copy(b, g).start)
            for s in range(sides if q < chunks else 0):
                guarded(side_there(s), mid_copy(s, g).start)

    for i in range(WINDOW):
        send_halo(i)

    for b in range(2):
        def clear(b=b):
            at = b * (edge + tokens)
            main[:, at : at + edge] = jnp.zeros((2, edge, width), BF16)
            rim_in[b] = jnp.zeros(rim_in.shape[1:], BF16)
        pl.when(jnp.logical_not(row_there(b)))(clear)
    for s in range(sides):
        if sides == 2:
            def clear_side(s=s):
                for ref in (mid, corner, crim_in, mrim_in):
                    ref[s] = jnp.zeros(ref.shape[1:], BF16)
            pl.when(jnp.logical_not(side_there(s)))(clear_side)

    for k in range(2):
        main[k, edge : edge + tokens] = kv_ref[k]

    got_rows[r] = jnp.zeros(got_rows.shape[1:], BF16)
    d_att[...] = mm(og_ref[...], w_ref[...], 1, 1).astype(BF16)
    acc[...] = jnp.zeros(acc.shape, F32)

    def put_bias(b, at, rows, cols, n):
        lane = lax.broadcasted_iota(jnp.int32, (n, step), 1)
        q_row = r * tile_h + b * QB + lane // tile_w
        q_col = c * tile_w + lane % tile_w
        first_r = jnp.clip(q_row - RAD, 0, image_h - WIN)
        first_c = jnp.clip(q_col - RAD, 0, image_w - WIN)
        ok = (rows >= first_r) & (rows < first_r + WIN) & (cols >= first_c) & (cols < first_c + WIN)
        bias[b, at : at + n] = jnp.where(ok, 0.0, -1e30)

    for b in range(blocks):
        token = lax.broadcasted_iota(jnp.int32, (span, step), 0)
        put_bias(b, 0, r * tile_h + b * QB - RAD + token // tile_w, c * tile_w + token % tile_w, span)
        for s in range(sides):
            if sides == 1:
                first = c * tile_w + jnp.where(c == 0, tile_w, -RAD)
            else:
                first = c * tile_w + (tile_w if s else -RAD)
            at = span + s * sspan
            token = lax.broadcasted_iota(jnp.int32, (CORNER, step), 0)
            row = (token * 10923) >> 16
            tall = jnp.where(token < RAD * RAD, row + (tile_h if b else -RAD), 2 * image_h)
            put_bias(b, at, r * tile_h + tall, first + token - row * RAD, CORNER)
            token = lax.broadcasted_iota(jnp.int32, (strip, step), 0)
            row = (token * 10923) >> 16
            put_bias(b, at + CORNER, r * tile_h + row, first + token - row * RAD, strip)

    def lanes(p):
        return pl.ds(pl.multiple_of(p * PAIR, PAIR), PAIR)

    def block_rows(b):
        return pl.ds(pl.multiple_of(b * step, step), span)

    def keys_of(k, b, p):
        parts = [main[k, block_rows(b), lanes(p)]]
        for s in range(sides):
            parts.append(corner[s, b, k, :, lanes(p)])
            parts.append(mid[s, k, :, lanes(p)])
        return jnp.concatenate(parts, axis=0)

    def split_heads(x):
        low_head = lax.broadcasted_iota(jnp.int32, x.shape, 1) < HD
        wide = x.astype(F32)
        return jnp.concatenate(
            [jnp.where(low_head, wide, 0.0), jnp.where(low_head, 0.0, wide)], axis=0
        ).astype(BF16)

    def queries_of(here, p):
        return split_heads(q_ref[here, lanes(p)].astype(F32) * scale)

    def own_heads(x):
        return jnp.concatenate([x[:HD, :step], x[HD:, step:]], axis=0)

    def attend(n, p):
        b = phases[n]
        here = pl.ds(pl.multiple_of(b * step, step), step)
        keys, values = keys_of(0, b, p), keys_of(1, b, p)
        q_two = queries_of(here, p)
        d_blk = d_att[here, lanes(p)]
        d_two = split_heads(d_blk)
        hidden = bias[b]
        scores = mm(keys, q_two, 1, 1) + jnp.concatenate([hidden, hidden], axis=1)
        expd = jnp.exp(scores - jnp.max(scores, axis=0, keepdims=True))
        full = expd * (1.0 / jnp.sum(expd, axis=0, keepdims=True))
        low = full.astype(BF16)
        att = own_heads(mm(values, low, 0, 0)).astype(BF16)
        att_t[lanes(p), here] = att
        both = d_blk.astype(F32).T * att.astype(F32)
        delta = jnp.concatenate(
            [
                jnp.sum(both[:HD], axis=0, keepdims=True),
                jnp.sum(both[HD:], axis=0, keepdims=True),
            ],
            axis=1,
        )
        dscores = (full * (mm(values, d_two, 1, 1) - delta)).astype(BF16)
        dq = own_heads(mm(keys, dscores, 0, 0)) * scale
        dq_ref[here, lanes(p)] = dq.T.astype(BF16)
        for k, grad in ((0, mm(dscores, q_two, 1, 0)), (1, mm(low, d_two, 1, 0))):
            acc[k, block_rows(b), lanes(p)] += grad[:span]
            for s in range(sides):
                at = span + s * sspan
                crim_out[s, b, k, :, lanes(p)] = grad[at : at + CORNER].astype(BF16)
                rest = grad[at + CORNER : at + sspan]
                if n == 0:
                    macc[s, k, :, lanes(p)] = rest
                else:
                    mrim_out[s, k, :, lanes(p)] = (macc[s, k, :, lanes(p)] + rest).astype(BF16)

    block_c = slab.shape[3]
    rows_c = width // n_rows
    og = og_ref[...]

    def dp_copy(k, g):
        to = lax.rem(d + k, n_dp)
        at = pl.ds(g * part, part)
        return pltpu.make_async_remote_copy(
            src_ref=slab_low.at[to, :, at], dst_ref=got_dp.at[k - 1, :, at],
            send_sem=dp_sems.at[0, k - 1, g], recv_sem=dp_sems.at[1, k - 1, g],
            device_id={"dp": to}, device_id_type=MESH,
        )

    def cols_copy(k, g):
        to = lax.rem(c + k, n_cols)
        at = pl.ds(g * part, part)
        return pltpu.make_async_remote_copy(
            src_ref=low_cols.at[to, at], dst_ref=got_cols.at[k - 1, at],
            send_sem=cols_sems.at[0, k - 1, g], recv_sem=cols_sems.at[1, k - 1, g],
            device_id={"cols": to}, device_id_type=MESH,
        )

    def rows_copy(to):
        return pltpu.make_async_remote_copy(
            src_ref=low_rows.at[to], dst_ref=got_rows.at[r],
            send_sem=rows_sems.at[0, to], recv_sem=rows_sems.at[1, r],
            device_id={"rows": to}, device_id_type=MESH,
        )

    def rows_arrival(source):
        return pltpu.make_async_remote_copy(
            src_ref=low_rows.at[source], dst_ref=got_rows.at[source],
            send_sem=rows_sems.at[0, source], recv_sem=rows_sems.at[1, source],
            device_id={"rows": source}, device_id_type=MESH,
        )

    def product(g):
        at = slice(g * part, (g + 1) * part)
        left = att_t[at]
        for j in range(n_cols):
            for e in range(n_dp):
                first = (j * n_dp + e) * block_c
                term = mm(left, og[:, first : first + block_c], 1, 0)
                slab[e, j, at] = term
                slab_low[e, j, at] = term.astype(BF16)
        for k in range(1, n_dp):
            dp_copy(k, g).start()

    def sum_dp(g):
        at = slice(g * part, (g + 1) * part)
        for k in range(1, n_dp):
            dp_copy(k, g).wait()
        for j in range(n_cols):
            total = slab[d, j, at]
            for k in range(1, n_dp):
                total = total + got_dp[k - 1, j, at].astype(F32)
            slab[d, j, at] = total
            low_cols[j, at] = total.astype(BF16)
        for k in range(1, n_cols):
            cols_copy(k, g).start()

    def sum_cols(g):
        at = slice(g * part, (g + 1) * part)
        for k in range(1, n_cols):
            cols_copy(k, g).wait()
        total = slab[d, c, at]
        for k in range(1, n_cols):
            total = total + got_cols[k - 1, at].astype(F32)
        slab[d, c, at] = total
        for i in range(part // rows_c):
            to = g * part // rows_c + i
            low_rows[to] = total[i * rows_c : (i + 1) * rows_c].astype(BF16)
            pl.when(r != to)(rows_copy(to).start)

    def wg_step(n):
        for level, sums in ((1, sum_cols), (0, sum_dp)):
            if 0 <= n - LAGS[level] < chunks:
                sums(turn[n - LAGS[level]])

    def send_corners(i):
        b, g = phases[seq[i] // chunks], turn[seq[i] % chunks]
        at = lanes_of(g)
        pl.when(row_there(b))(lambda: halo_arrival(b, g).wait_recv())
        send_halo(i + WINDOW)
        for s in range(sides):
            for k in range(2):
                own_corner[s, b, k, :, at] = mm(pick_corner[s], main[k, halo_rows(b), at], 1, 0).astype(BF16)
            guarded(side_there(s), corner_copy(s, b, g).start)

    def wait_sides(n, g):
        for s in range(sides):
            def arrived(s=s):
                if n == 0:
                    mid_arrival(s, g).wait_recv()
                corner_arrival(s, phases[n], g).wait_recv()
            guarded(side_there(s), arrived)

    def send_sides(n, g):
        for s in range(sides):
            def send(s=s):
                crim_copy(s, phases[n], g).start()
                if n == 1:
                    mrim_copy(s, g).start()
            guarded(side_there(s), send)

    def send_rims(n, g):
        b, at = phases[n], lanes_of(g)
        for s in range(sides):
            guarded(side_there(s), lambda s=s: crim_arrival(s, b, g).wait_recv())
        for k in range(2):
            total = acc[k, halo_rows(b), at]
            for s in range(sides):
                total = total + mm(put_corner[s], crim_in[s, b, k, :, at], 1, 0)
            rim_out[b, k, :, at] = total.astype(BF16)
        pl.when(row_there(b))(rim_copy(b, g).start)

    def finish(g):
        at = lanes_of(g)
        for s in range(sides):
            guarded(side_there(s), lambda s=s: mrim_arrival(s, g).wait_recv())
        for b in range(2):
            pl.when(row_there(b))(lambda b=b: rim_arrival(b, g).wait_recv())
        for k in range(2):
            own = acc[k, edge : edge + tokens, at]
            for s in range(sides):
                own = own + mm(put_mid[s], mrim_in[s, k, :, at], 1, 0)
            kvg_ref[k, edge : tokens - edge, at] = own[edge : tokens - edge].astype(BF16)
            kvg_ref[k, :edge, at] = (own[:edge] + rim_in[0, k, :, at].astype(F32)).astype(BF16)
            kvg_ref[k, tokens - edge :, at] = (own[tokens - edge :] + rim_in[1, k, :, at].astype(F32)).astype(BF16)

    steps = 2 * chunks
    rims = [*seq]

    def flush_rims(count):
        for _ in range(count):
            q = rims.pop(0)
            send_rims(q // chunks, turn[q % chunks])

    for q in range(AHEAD):
        send_corners(q)
    for at, q in enumerate(seq):
        n, g = q // chunks, turn[q % chunks]
        if at + AHEAD < steps:
            send_corners(at + AHEAD)
        wait_sides(n, g)
        attend(n, g)
        send_sides(n, g)
        if n == 1:
            product(g)
            wg_step(q - chunks)
        if at >= HOLD:
            flush_rims(RATE)
    n = chunks
    while rims or n < chunks + WG_TAIL:
        if n < chunks + WG_TAIL:
            wg_step(n)
            n += 1
        flush_rims(min(len(rims), RATE))
    out_ref[...] = mm(att_t[...], w_ref[...], 0, 0).astype(BF16)
    for i in range(chunks):
        if n < chunks + LAGS[1]:
            wg_step(n)
            n += 1
        finish(turn[i])
    while n < chunks + LAGS[1]:
        wg_step(n)
        n += 1

    for g in range(chunks):
        for b in range(2):
            def sent(b=b, g=g):
                halo_copy(b, g).wait_send()
                rim_copy(b, g).wait_send()
            pl.when(row_there(b))(sent)
        for s in range(sides):
            def side_sent(s=s, g=g):
                mid_copy(s, g).wait_send()
                mrim_copy(s, g).wait_send()
                for b in range(2):
                    corner_copy(s, b, g).wait_send()
                    crim_copy(s, b, g).wait_send()
            guarded(side_there(s), side_sent)
    for source in range(n_rows):
        def collect(source=source):
            rows_arrival(source).wait_recv()
            rows_copy(source).wait_send()
        pl.when(r != source)(collect)
    total = slab[d, c, pl.ds(pl.multiple_of(r * rows_c, rows_c), rows_c)]
    for source in range(n_rows):
        total = total + got_rows[source].astype(F32)
    wg_ref[...] = total * (1.0 / math.sqrt(image_h * image_w * n_dp))


def local(n_rows, n_cols, n_dp, queries, keys_values, out_weight, out_grad):
    tile_h, tile_w, width = queries.shape[1:]
    tokens = tile_h * tile_w
    sides = 1 if n_cols == 2 else 2
    blocks = tile_h // QB
    pairs = width // PAIR
    edge = RAD * tile_w
    grown = tokens + 2 * edge
    strip = tile_h * RAD
    seen = (QB + 2 * RAD) * tile_w + sides * (CORNER + strip)
    step = QB * tile_w
    block_c = width // (n_cols * n_dp)
    rows_c = width // n_rows
    chunks = pairs // CHUNK
    vmem = pl.BlockSpec(memory_space=pltpu.VMEM)
    dma = pltpu.SemaphoreType.DMA
    shapes = (
        jax.ShapeDtypeStruct((tokens, width), BF16),
        jax.ShapeDtypeStruct((tokens, width), BF16),
        jax.ShapeDtypeStruct((2, tokens, width), BF16),
        jax.ShapeDtypeStruct((rows_c, block_c), F32),
    )
    results = pl.pallas_call(
        functools.partial(kernel, tile_h, tile_w, n_rows, n_cols, n_dp),
        out_shape=tuple(pltpu.VMEM(x.shape, x.dtype) for x in shapes),
        in_specs=[vmem] * 4,
        out_specs=(vmem,) * 4,
        scratch_shapes=[
            pltpu.VMEM((2, grown, width), BF16),
            pltpu.VMEM((sides, 2, 2, CORNER, width), BF16),
            pltpu.VMEM((sides, 2, 2, CORNER, width), BF16),
            pltpu.VMEM((sides, 2, strip, width), BF16),
            pltpu.VMEM((sides, 2, strip, width), BF16),
            pltpu.VMEM((2, grown, width), F32),
            pltpu.VMEM((sides, 2, strip, width), F32),
            pltpu.VMEM((blocks, seen, step), F32),
            pltpu.VMEM((width, tokens), BF16),
            pltpu.VMEM((tokens, width), BF16),
            pltpu.VMEM((2, 2, edge, width), BF16),
            pltpu.VMEM((2, 2, edge, width), BF16),
            pltpu.VMEM((sides, 2, 2, CORNER, width), BF16),
            pltpu.VMEM((sides, 2, 2, CORNER, width), BF16),
            pltpu.VMEM((sides, 2, strip, width), BF16),
            pltpu.VMEM((sides, 2, strip, width), BF16),
            pltpu.VMEM((n_dp, n_cols, width, block_c), F32),
            pltpu.VMEM((n_dp, n_cols, width, block_c), BF16),
            pltpu.VMEM((n_dp - 1, n_cols, width, block_c), BF16),
            pltpu.VMEM((n_cols, width, block_c), BF16),
            pltpu.VMEM((n_cols - 1, width, block_c), BF16),
            pltpu.VMEM((n_rows, rows_c, block_c), BF16),
            pltpu.VMEM((n_rows, rows_c, block_c), BF16),
            dma((2, 2, chunks)), dma((2, sides, chunks)), dma((2, sides, 2, chunks)),
            dma((2, 2, chunks)), dma((2, sides, 2, chunks)), dma((2, sides, chunks)),
            dma((2, n_dp - 1, chunks)), dma((2, n_cols - 1, chunks)), dma((2, n_rows)),
        ],
        compiler_params=pltpu.CompilerParams(
            collective_id=0, has_side_effects=True, vmem_limit_bytes=60 * 2**20
        ),
    )(
        queries.reshape(tokens, width),
        keys_values.reshape(2, tokens, width),
        out_weight,
        out_grad.reshape(tokens, width),
    )
    out, dq, kvg, wg = results
    return (
        out.reshape(queries.shape),
        dq.reshape(queries.shape),
        kvg.reshape(keys_values.shape),
        wg,
    )


def solution(mesh):
    in_specs = (
        P("dp", "rows", "cols", None),
        P(None, "dp", "rows", "cols", None),
        P(),
        P("dp", "rows", "cols", None),
    )
    out_specs = (
        P("dp", "rows", "cols", None),
        P("dp", "rows", "cols", None),
        P(None, "dp", "rows", "cols", None),
        P("rows", ("cols", "dp")),
    )
    sizes = (mesh.shape["rows"], mesh.shape["cols"], mesh.shape["dp"])
    return jax.shard_map(
        functools.partial(local, *sizes),
        mesh=mesh, in_specs=in_specs, out_specs=out_specs, check_vma=False,
    )
```

```python
import functools
import math

import jax
import jax.numpy as jnp
from jax import lax
from jax.experimental import pallas as pl
from jax.experimental.pallas import tpu as pltpu
from jax.sharding import PartitionSpec as P

NH = 16
HD = 64
RAD = 6
WIN = 13
QB = 8
PAIR = 2 * HD
CHUNK = 1
CORNER = -(-RAD * RAD // 16) * 16
AHEAD = 6
WINDOW = 8
HOLD = 4
SHIFT = 6
RATE = 1
WG_TAIL = 3
LAGS = (3, 8)
MESH = pl.DeviceIdType.MESH
F32 = jnp.float32
BF16 = jnp.bfloat16


def mm(a, b, ca, cb):
    return lax.dot_general(a, b, (((ca,), (cb,)), ((), ())), preferred_element_type=F32)


def kernel(
    tile_h, tile_w, n_rows, n_cols, n_dp,
    q_ref, kv_ref, w_ref, og_ref,
    out_ref, dq_ref, kvg_ref, wg_ref,
    main, corner, own_corner, mid, own_mid, acc, macc, bias, att_t, d_att,
    rim_out, rim_in, crim_out, crim_in, mrim_out, mrim_in,
    slab, slab_low, got_dp, low_cols, got_cols, low_rows, got_rows,
    halo_sems, mid_sems, corner_sems, rim_sems, crim_sems, mrim_sems, dp_sems, cols_sems, rows_sems,
):
    sides = mid.shape[0]
    blocks = tile_h // QB
    tokens = tile_h * tile_w
    width = q_ref.shape[1]
    pairs = width // PAIR
    edge = RAD * tile_w
    span = (QB + 2 * RAD) * tile_w
    strip = tile_h * RAD
    sspan = CORNER + strip
    step = QB * tile_w
    image_h, image_w = tile_h * n_rows, tile_w * n_cols
    scale = 1.0 / math.sqrt(HD)
    r, c, d = lax.axis_index("rows"), lax.axis_index("cols"), lax.axis_index("dp")
    chunks = pairs // CHUNK
    turn = [g for h in range(2) for g in (h, chunks - 2 + h, 2 + h, chunks - 4 + h)] if chunks == 8 else [*range(chunks)]
    part = CHUNK * PAIR
    seq = [n * chunks + t - n * SHIFT for t in range(chunks + SHIFT) for n in range(2) if 0 <= t - n * SHIFT < chunks]
    first_b = lax.rem(r, 2)
    phases = (first_b, 1 - first_b)

    def lanes_of(g):
        return pl.ds(g * part, part)

    def row_there(b):
        return (r + 2 * b > 0) & (r + 2 * b < n_rows + 1)

    def side_there(s):
        if sides == 1:
            return None
        return c > 0 if s == 0 else c < n_cols - 1

    def guarded(ok, action):
        if ok is None:
            action()
        else:
            pl.when(ok)(action)

    def side_col(s):
        return 1 - c if sides == 1 else c + (2 * s - 1)

    def slot(s):
        return 0 if sides == 1 else 1 - s

    def starts_at(s):
        if sides == 1:
            return (1 - c) * (tile_w - RAD)
        return 0 if s == 0 else tile_w - RAD

    barrier = pltpu.get_barrier_semaphore()
    for k in range(1, n_rows):
        pl.semaphore_signal(barrier, 1, device_id={"rows": lax.rem(r + k, n_rows)}, device_id_type=MESH)
    for k in range(1, n_cols):
        pl.semaphore_signal(barrier, 1, device_id={"cols": lax.rem(c + k, n_cols)}, device_id_type=MESH)
    for k in range(1, n_dp):
        pl.semaphore_signal(barrier, 1, device_id={"dp": lax.rem(d + k, n_dp)}, device_id_type=MESH)

    pl.semaphore_wait(barrier, n_rows + n_cols + n_dp - 3)

    def place(token, s):
        row = (token * 10923) >> 16
        return row * tile_w + token - row * RAD + starts_at(s)

    def one_hot(n, cells, used, s, token_axis):
        shape = (n, cells) if token_axis == 0 else (cells, n)
        token = lax.broadcasted_iota(jnp.int32, shape, token_axis)
        cell = lax.broadcasted_iota(jnp.int32, shape, 1 - token_axis)
        return ((place(token, s) == cell) & (token < used)).astype(F32).astype(BF16)

    pick_corner = [one_hot(CORNER, edge, RAD * RAD, s, 0) for s in range(sides)]
    put_corner = [one_hot(CORNER, edge, RAD * RAD, s, 1) for s in range(sides)]
    put_mid = [one_hot(strip, tokens, strip, s, 1) for s in range(sides)]

    def row_link(b, src, dst, sems, g):
        return pltpu.make_async_remote_copy(
            src_ref=src, dst_ref=dst, send_sem=sems.at[0, b, g], recv_sem=sems.at[1, 1 - b, g],
            device_id={"rows": r + 2 * b - 1}, device_id_type=MESH,
        )

    def row_arrival(b, dst, sems, g):
        return pltpu.make_async_remote_copy(
            src_ref=dst, dst_ref=dst, send_sem=sems.at[0, b, g], recv_sem=sems.at[1, b, g],
            device_id={"rows": r + 2 * b - 1}, device_id_type=MESH,
        )

    def halo_rows(b):
        return pl.ds(pl.multiple_of(b * (edge + tokens), 16), edge)

    def halo_place(b, g):
        return main.at[:, halo_rows(b), lanes_of(g)]

    def halo_copy(b, g):
        own = kv_ref.at[:, pl.ds(pl.multiple_of(b * (tokens - edge), 16), edge), lanes_of(g)]
        return row_link(b, own, halo_place(1 - b, g), halo_sems, g)

    def halo_arrival(b, g):
        return row_arrival(b, halo_place(b, g), halo_sems, g)

    def rim_copy(b, g):
        at = lanes_of(g)
        return row_link(b, rim_out.at[b, :, :, at], rim_in.at[1 - b, :, :, at], rim_sems, g)

    def rim_arrival(b, g):
        return row_arrival(b, rim_in.at[b, :, :, lanes_of(g)], rim_sems, g)

    def side_copy(s, src, dst, send, recv):
        return pltpu.make_async_remote_copy(
            src_ref=src, dst_ref=dst, send_sem=send, recv_sem=recv,
            device_id={"cols": side_col(s)}, device_id_type=MESH,
        )

    def mid_copy(s, g, src=own_mid, dst=mid, sems=mid_sems):
        at, far = lanes_of(g), slot(s)
        return side_copy(s, src.at[s, :, :, at], dst.at[far, :, :, at], sems.at[0, s, g], sems.at[1, far, g])

    def mid_arrival(s, g, dst=mid, sems=mid_sems):
        at = dst.at[s, :, :, lanes_of(g)]
        return side_copy(s, at, at, sems.at[0, s, g], sems.at[1, s, g])

    def corner_copy(s, b, g, src=own_corner, dst=corner, sems=corner_sems):
        at, far = lanes_of(g), slot(s)
        return side_copy(
            s, src.at[s, b, :, :, at], dst.at[far, b, :, :, at], sems.at[0, s, b, g], sems.at[1, far, b, g]
        )

    def corner_arrival(s, b, g, dst=corner, sems=corner_sems):
        at = dst.at[s, b, :, :, lanes_of(g)]
        return side_copy(s, at, at, sems.at[0, s, b, g], sems.at[1, s, b, g])

    def mrim_copy(s, g):
        return mid_copy(s, g, mrim_out, mrim_in, mrim_sems)

    def mrim_arrival(s, g):
        return mid_arrival(s, g, mrim_in, mrim_sems)

    def crim_copy(s, b, g):
        return corner_copy(s, b, g, crim_out, crim_in, crim_sems)

    def crim_arrival(s, b, g):
        return corner_arrival(s, b, g, crim_in, crim_sems)

    def send_halo(i):
        if i < 2 * chunks:
            q = seq[i]
            b, g = phases[q // chunks], turn[q % chunks]
            pl.when(row_there(b))(halo_copy(b, g).start)
            if i >= WINDOW:
                send_mid(i)

    def send_mid(i):
        for s in range(sides if seq[i] < chunks else 0):
            guarded(side_there(s), mid_copy(s, turn[seq[i] % chunks]).start)

    for i in range(WINDOW):
        send_halo(i)
    for s in range(sides):
        chosen = one_hot(strip, tokens, strip, s, 0)
        for k in range(2):
            own_mid[s, k] = mm(chosen, kv_ref[k], 1, 0).astype(BF16)
    for i in range(WINDOW):
        send_mid(i)

    for b in range(2):
        def clear(b=b):
            at = b * (edge + tokens)
            main[:, at : at + edge] = jnp.zeros((2, edge, width), BF16)
            rim_in[b] = jnp.zeros(rim_in.shape[1:], BF16)
        pl.when(jnp.logical_not(row_there(b)))(clear)
    for s in range(sides):
        if sides == 2:
            def clear_side(s=s):
                for ref in (mid, corner, crim_in, mrim_in):
                    ref[s] = jnp.zeros(ref.shape[1:], BF16)
            pl.when(jnp.logical_not(side_there(s)))(clear_side)

    for k in range(2):
        main[k, edge : edge + tokens] = kv_ref[k]

    got_rows[r] = jnp.zeros(got_rows.shape[1:], BF16)
    d_att[...] = mm(og_ref[...], w_ref[...], 1, 1).astype(BF16)
    acc[...] = jnp.zeros(acc.shape, F32)

    def put_bias(b, at, rows, cols, n):
        lane = lax.broadcasted_iota(jnp.int32, (n, step), 1)
        q_row = r * tile_h + b * QB + lane // tile_w
        q_col = c * tile_w + lane % tile_w
        first_r = jnp.clip(q_row - RAD, 0, image_h - WIN)
        first_c = jnp.clip(q_col - RAD, 0, image_w - WIN)
        ok = (rows >= first_r) & (rows < first_r + WIN) & (cols >= first_c) & (cols < first_c + WIN)
        bias[b, at : at + n] = jnp.where(ok, 0.0, -1e30)

    for b in range(blocks):
        token = lax.broadcasted_iota(jnp.int32, (span, step), 0)
        put_bias(b, 0, r * tile_h + b * QB - RAD + token // tile_w, c * tile_w + token % tile_w, span)
        for s in range(sides):
            if sides == 1:
                first = c * tile_w + jnp.where(c == 0, tile_w, -RAD)
            else:
                first = c * tile_w + (tile_w if s else -RAD)
            at = span + s * sspan
            token = lax.broadcasted_iota(jnp.int32, (CORNER, step), 0)
            row = (token * 10923) >> 16
            tall = jnp.where(token < RAD * RAD, row + (tile_h if b else -RAD), 2 * image_h)
            put_bias(b, at, r * tile_h + tall, first + token - row * RAD, CORNER)
            token = lax.broadcasted_iota(jnp.int32, (strip, step), 0)
            row = (token * 10923) >> 16
            put_bias(b, at + CORNER, r * tile_h + row, first + token - row * RAD, strip)

    def lanes(p):
        return pl.ds(pl.multiple_of(p * PAIR, PAIR), PAIR)

    def block_rows(b):
        return pl.ds(pl.multiple_of(b * step, step), span)

    def keys_of(k, b, p):
        parts = [main[k, block_rows(b), lanes(p)]]
        for s in range(sides):
            parts.append(corner[s, b, k, :, lanes(p)])
            parts.append(mid[s, k, :, lanes(p)])
        return jnp.concatenate(parts, axis=0)

    def split_heads(x):
        low_head = lax.broadcasted_iota(jnp.int32, x.shape, 1) < HD
        wide = x.astype(F32)
        return jnp.concatenate(
            [jnp.where(low_head, wide, 0.0), jnp.where(low_head, 0.0, wide)], axis=0
        ).astype(BF16)

    def queries_of(here, p):
        return split_heads(q_ref[here, lanes(p)].astype(F32) * scale)

    def own_heads(x):
        return jnp.concatenate([x[:HD, :step], x[HD:, step:]], axis=0)

    def attend(n, p):
        b = phases[n]
        here = pl.ds(pl.multiple_of(b * step, step), step)
        keys, values = keys_of(0, b, p), keys_of(1, b, p)
        q_two = queries_of(here, p)
        d_blk = d_att[here, lanes(p)]
        d_two = split_heads(d_blk)
        hidden = bias[b]
        scores = mm(keys, q_two, 1, 1) + jnp.concatenate([hidden, hidden], axis=1)
        expd = jnp.exp(scores - jnp.max(scores, axis=0, keepdims=True))
        full = expd * (1.0 / jnp.sum(expd, axis=0, keepdims=True))
        low = full.astype(BF16)
        att = own_heads(mm(values, low, 0, 0)).astype(BF16)
        att_t[lanes(p), here] = att
        both = d_blk.astype(F32).T * att.astype(F32)
        delta = jnp.concatenate(
            [
                jnp.sum(both[:HD], axis=0, keepdims=True),
                jnp.sum(both[HD:], axis=0, keepdims=True),
            ],
            axis=1,
        )
        dscores = (full * (mm(values, d_two, 1, 1) - delta)).astype(BF16)
        dq = own_heads(mm(keys, dscores, 0, 0)) * scale
        dq_ref[here, lanes(p)] = dq.T.astype(BF16)
        for k, grad in ((0, mm(dscores, q_two, 1, 0)), (1, mm(low, d_two, 1, 0))):
            acc[k, block_rows(b), lanes(p)] += grad[:span]
            for s in range(sides):
                at = span + s * sspan
                crim_out[s, b, k, :, lanes(p)] = grad[at : at + CORNER].astype(BF16)
                rest = grad[at + CORNER : at + sspan]
                if n == 0:
                    macc[s, k, :, lanes(p)] = rest
                else:
                    mrim_out[s, k, :, lanes(p)] = (macc[s, k, :, lanes(p)] + rest).astype(BF16)

    block_c = slab.shape[3]
    rows_c = width // n_rows
    og = og_ref[...]

    def dp_copy(k, g):
        to = lax.rem(d + k, n_dp)
        at = pl.ds(g * part, part)
        return pltpu.make_async_remote_copy(
            src_ref=slab_low.at[to, :, at], dst_ref=got_dp.at[k - 1, :, at],
            send_sem=dp_sems.at[0, k - 1, g], recv_sem=dp_sems.at[1, k - 1, g],
            device_id={"dp": to}, device_id_type=MESH,
        )

    def cols_copy(k, g):
        to = lax.rem(c + k, n_cols)
        at = pl.ds(g * part, part)
        return pltpu.make_async_remote_copy(
            src_ref=low_cols.at[to, at], dst_ref=got_cols.at[k - 1, at],
            send_sem=cols_sems.at[0, k - 1, g], recv_sem=cols_sems.at[1, k - 1, g],
            device_id={"cols": to}, device_id_type=MESH,
        )

    def rows_copy(to):
        return pltpu.make_async_remote_copy(
            src_ref=low_rows.at[to], dst_ref=got_rows.at[r],
            send_sem=rows_sems.at[0, to], recv_sem=rows_sems.at[1, r],
            device_id={"rows": to}, device_id_type=MESH,
        )

    def rows_arrival(source):
        return pltpu.make_async_remote_copy(
            src_ref=low_rows.at[source], dst_ref=got_rows.at[source],
            send_sem=rows_sems.at[0, source], recv_sem=rows_sems.at[1, source],
            device_id={"rows": source}, device_id_type=MESH,
        )

    def product(g):
        at = slice(g * part, (g + 1) * part)
        left = att_t[at]
        for j in range(n_cols):
            for e in range(n_dp):
                first = (j * n_dp + e) * block_c
                term = mm(left, og[:, first : first + block_c], 1, 0)
                slab[e, j, at] = term
                slab_low[e, j, at] = term.astype(BF16)
        for k in range(1, n_dp):
            dp_copy(k, g).start()

    def sum_dp(g):
        at = slice(g * part, (g + 1) * part)
        for k in range(1, n_dp):
            dp_copy(k, g).wait()
        for j in range(n_cols):
            total = slab[d, j, at]
            for k in range(1, n_dp):
                total = total + got_dp[k - 1, j, at].astype(F32)
            slab[d, j, at] = total
            low_cols[j, at] = total.astype(BF16)
        for k in range(1, n_cols):
            cols_copy(k, g).start()

    def sum_cols(g):
        at = slice(g * part, (g + 1) * part)
        for k in range(1, n_cols):
            cols_copy(k, g).wait()
        total = slab[d, c, at]
        for k in range(1, n_cols):
            total = total + got_cols[k - 1, at].astype(F32)
        slab[d, c, at] = total
        for i in range(part // rows_c):
            to = g * part // rows_c + i
            low_rows[to] = total[i * rows_c : (i + 1) * rows_c].astype(BF16)
            pl.when(r != to)(rows_copy(to).start)

    def wg_step(n):
        for level, sums in ((1, sum_cols), (0, sum_dp)):
            if 0 <= n - LAGS[level] < chunks:
                sums(turn[n - LAGS[level]])

    def send_corners(i):
        b, g = phases[seq[i] // chunks], turn[seq[i] % chunks]
        at = lanes_of(g)
        pl.when(row_there(b))(lambda: halo_arrival(b, g).wait_recv())
        send_halo(i + WINDOW)
        for s in range(sides):
            for k in range(2):
                own_corner[s, b, k, :, at] = mm(pick_corner[s], main[k, halo_rows(b), at], 1, 0).astype(BF16)
            guarded(side_there(s), corner_copy(s, b, g).start)

    def wait_sides(n, g):
        for s in range(sides):
            def arrived(s=s):
                if n == 0:
                    mid_arrival(s, g).wait_recv()
                corner_arrival(s, phases[n], g).wait_recv()
            guarded(side_there(s), arrived)

    def send_sides(n, g):
        for s in range(sides):
            def send(s=s):
                crim_copy(s, phases[n], g).start()
                if n == 1:
                    mrim_copy(s, g).start()
            guarded(side_there(s), send)

    def send_rims(n, g):
        b, at = phases[n], lanes_of(g)
        for s in range(sides):
            guarded(side_there(s), lambda s=s: crim_arrival(s, b, g).wait_recv())
        for k in range(2):
            total = acc[k, halo_rows(b), at]
            for s in range(sides):
                total = total + mm(put_corner[s], crim_in[s, b, k, :, at], 1, 0)
            rim_out[b, k, :, at] = total.astype(BF16)
        pl.when(row_there(b))(rim_copy(b, g).start)

    def finish(g):
        at = lanes_of(g)
        for s in range(sides):
            guarded(side_there(s), lambda s=s: mrim_arrival(s, g).wait_recv())
        for b in range(2):
            pl.when(row_there(b))(lambda b=b: rim_arrival(b, g).wait_recv())
        for k in range(2):
            own = acc[k, edge : edge + tokens, at]
            for s in range(sides):
                own = own + mm(put_mid[s], mrim_in[s, k, :, at], 1, 0)
            kvg_ref[k, edge : tokens - edge, at] = own[edge : tokens - edge].astype(BF16)
            kvg_ref[k, :edge, at] = (own[:edge] + rim_in[0, k, :, at].astype(F32)).astype(BF16)
            kvg_ref[k, tokens - edge :, at] = (own[tokens - edge :] + rim_in[1, k, :, at].astype(F32)).astype(BF16)

    steps = 2 * chunks
    rims = [*seq]

    def flush_rims(count):
        for _ in range(count):
            q = rims.pop(0)
            send_rims(q // chunks, turn[q % chunks])

    for q in range(AHEAD):
        send_corners(q)
    for at, q in enumerate(seq):
        n, g = q // chunks, turn[q % chunks]
        if at + AHEAD < steps:
            send_corners(at + AHEAD)
        wait_sides(n, g)
        attend(n, g)
        send_sides(n, g)
        if n == 1:
            product(g)
            wg_step(q - chunks)
        if at >= HOLD:
            flush_rims(RATE)
    n = chunks
    while rims or n < chunks + WG_TAIL:
        if n < chunks + WG_TAIL:
            wg_step(n)
            n += 1
        flush_rims(min(len(rims), RATE))
    out_ref[...] = mm(att_t[...], w_ref[...], 0, 0).astype(BF16)
    for i in range(chunks):
        if n < chunks + LAGS[1]:
            wg_step(n)
            n += 1
        finish(turn[i])
    while n < chunks + LAGS[1]:
        wg_step(n)
        n += 1

    for g in range(chunks):
        for b in range(2):
            def sent(b=b, g=g):
                halo_copy(b, g).wait_send()
                rim_copy(b, g).wait_send()
            pl.when(row_there(b))(sent)
        for s in range(sides):
            def side_sent(s=s, g=g):
                mid_copy(s, g).wait_send()
                mrim_copy(s, g).wait_send()
                for b in range(2):
                    corner_copy(s, b, g).wait_send()
                    crim_copy(s, b, g).wait_send()
            guarded(side_there(s), side_sent)
    for source in range(n_rows):
        def collect(source=source):
            rows_arrival(source).wait_recv()
            rows_copy(source).wait_send()
        pl.when(r != source)(collect)
    total = slab[d, c, pl.ds(pl.multiple_of(r * rows_c, rows_c), rows_c)]
    for source in range(n_rows):
        total = total + got_rows[source].astype(F32)
    wg_ref[...] = total * (1.0 / math.sqrt(image_h * image_w * n_dp))


def local(n_rows, n_cols, n_dp, queries, keys_values, out_weight, out_grad):
    tile_h, tile_w, width = queries.shape[1:]
    tokens = tile_h * tile_w
    sides = 1 if n_cols == 2 else 2
    blocks = tile_h // QB
    pairs = width // PAIR
    edge = RAD * tile_w
    grown = tokens + 2 * edge
    strip = tile_h * RAD
    seen = (QB + 2 * RAD) * tile_w + sides * (CORNER + strip)
    step = QB * tile_w
    block_c = width // (n_cols * n_dp)
    rows_c = width // n_rows
    chunks = pairs // CHUNK
    vmem = pl.BlockSpec(memory_space=pltpu.VMEM)
    dma = pltpu.SemaphoreType.DMA
    shapes = (
        jax.ShapeDtypeStruct((tokens, width), BF16),
        jax.ShapeDtypeStruct((tokens, width), BF16),
        jax.ShapeDtypeStruct((2, tokens, width), BF16),
        jax.ShapeDtypeStruct((rows_c, block_c), F32),
    )
    results = pl.pallas_call(
        functools.partial(kernel, tile_h, tile_w, n_rows, n_cols, n_dp),
        out_shape=tuple(pltpu.VMEM(x.shape, x.dtype) for x in shapes),
        in_specs=[vmem] * 4,
        out_specs=(vmem,) * 4,
        scratch_shapes=[
            pltpu.VMEM((2, grown, width), BF16),
            pltpu.VMEM((sides, 2, 2, CORNER, width), BF16),
            pltpu.VMEM((sides, 2, 2, CORNER, width), BF16),
            pltpu.VMEM((sides, 2, strip, width), BF16),
            pltpu.VMEM((sides, 2, strip, width), BF16),
            pltpu.VMEM((2, grown, width), F32),
            pltpu.VMEM((sides, 2, strip, width), F32),
            pltpu.VMEM((blocks, seen, step), F32),
            pltpu.VMEM((width, tokens), BF16),
            pltpu.VMEM((tokens, width), BF16),
            pltpu.VMEM((2, 2, edge, width), BF16),
            pltpu.VMEM((2, 2, edge, width), BF16),
            pltpu.VMEM((sides, 2, 2, CORNER, width), BF16),
            pltpu.VMEM((sides, 2, 2, CORNER, width), BF16),
            pltpu.VMEM((sides, 2, strip, width), BF16),
            pltpu.VMEM((sides, 2, strip, width), BF16),
            pltpu.VMEM((n_dp, n_cols, width, block_c), F32),
            pltpu.VMEM((n_dp, n_cols, width, block_c), BF16),
            pltpu.VMEM((n_dp - 1, n_cols, width, block_c), BF16),
            pltpu.VMEM((n_cols, width, block_c), BF16),
            pltpu.VMEM((n_cols - 1, width, block_c), BF16),
            pltpu.VMEM((n_rows, rows_c, block_c), BF16),
            pltpu.VMEM((n_rows, rows_c, block_c), BF16),
            dma((2, 2, chunks)), dma((2, sides, chunks)), dma((2, sides, 2, chunks)),
            dma((2, 2, chunks)), dma((2, sides, 2, chunks)), dma((2, sides, chunks)),
            dma((2, n_dp - 1, chunks)), dma((2, n_cols - 1, chunks)), dma((2, n_rows)),
        ],
        compiler_params=pltpu.CompilerParams(
            collective_id=0, has_side_effects=True, vmem_limit_bytes=60 * 2**20
        ),
    )(
        queries.reshape(tokens, width),
        keys_values.reshape(2, tokens, width),
        out_weight,
        out_grad.reshape(tokens, width),
    )
    out, dq, kvg, wg = results
    return (
        out.reshape(queries.shape),
        dq.reshape(queries.shape),
        kvg.reshape(keys_values.shape),
        wg,
    )


def solution(mesh):
    in_specs = (
        P("dp", "rows", "cols", None),
        P(None, "dp", "rows", "cols", None),
        P(),
        P("dp", "rows", "cols", None),
    )
    out_specs = (
        P("dp", "rows", "cols", None),
        P("dp", "rows", "cols", None),
        P(None, "dp", "rows", "cols", None),
        P("rows", ("cols", "dp")),
    )
    sizes = (mesh.shape["rows"], mesh.shape["cols"], mesh.shape["dp"])
    return jax.shard_map(
        functools.partial(local, *sizes),
        mesh=mesh, in_specs=in_specs, out_specs=out_specs, check_vma=False,
    )
```
